32 devices in a mesh: ma: 8 (over z, core), row: 4 (over y, x).
Axes of the slice: x: 2, y: 2, z: 4, core: 2. Of those that a mesh axis runs over, the one named last changes fastest.
Arguments:
- seed_field: bfloat16 [4, 4, 2, 1024, 1024], P(None, 'row', None, 'ma'), may hold values from -6 to 6
- cotangent: bfloat16 [2, 4, 2, 1024, 1024], P(None, 'row', None, 'ma'), may hold values from -6 to 6
- step_size: float32 [1], replicated, may hold values from 0.25 to 1
- owner_list: int32 [1024], replicated, may hold values from 0 to 1023, as said below
Outputs:
- nonlinear: float32 [2, 4, 2, 1024, 1024], P(None, 'row', None, 'ma')
- seed_next: float32 [4, 4, 2, 1024, 1024], P(None, 'row', None, 'ma')
The draws below stay inside these ranges and needn't reach their ends.
Inputs may be any that keep to these rules, and one draw needn't show every extreme that they name: owner_list is a permutation of the wavenumbers; entries 128 d to 128 (d + 1) - 1 name the wavenumbers of owner d, and a block that holds m also holds 1023 - m.
All inputs are finite; a program needn't handle non-finite values.
Results may differ from the reference program's by a relative error of at most 0.0082.
Values may be sent and summed in bfloat16 or wider, within the bound.
No kernel may reach another device: no remote copies, remote signals or barrier semaphores. Data moves between devices by JAX's collectives and lax.ppermute only.
A program may use at most 128 MiB of HBM per device.

```python
import math
import jax
import jax.numpy as jnp
from jax import lax

WAVES = 1024
DEGREES = 1024
NLAT = 1024
NLON = 2048
RADII = 4
OWN = 128


def draw_owner_list(key, part):
    pair_ids = jax.random.permutation(key, WAVES // 2).astype(jnp.int32).reshape(-1, OWN // 2)
    owner_rows = jnp.concatenate([pair_ids, WAVES - 1 - pair_ids], axis=1)
    return owner_rows.reshape(WAVES)


def block_scale(rng, shape, split, smallest, largest):
    level = 1.0
    for position, shards_of in split:
        steps = jax.random.uniform(jax.random.fold_in(jax.random.fold_in(rng, 6), position), (shards_of,), jnp.float32, smallest / len(split), largest / len(split))
        level = level * jnp.repeat(jnp.exp(steps), shape[position] // shards_of).reshape((-1,) + (1,) * (len(shape) - 1 - position))
    return level


def gaussian(rng, extent, spread, limit, pieces=(), kind=jnp.bfloat16):
    factor_of = block_scale(rng, extent, pieces, -0.22, 0.18) if pieces else 1.0
    values = jax.random.normal(rng, extent, jnp.float32) * spread * factor_of
    return jnp.minimum(jnp.maximum(values, -limit), limit).astype(kind)


def setup_inputs(seed: int = 0) -> dict:
    splits = jax.random.split(jax.random.key(seed), 5)
    return {
        "seed_field": gaussian(splits[0], (4, RADII, 2, DEGREES, WAVES), 1.0, 6.0, ((1, 4), (3, 8))),
        "cotangent": gaussian(splits[1], (2, RADII, 2, WAVES, DEGREES), 1.0, 6.0, ((1, 4), (3, 8))),
        "step_size": jnp.clip(jnp.exp(jax.random.uniform(splits[2], (1,), jnp.float32, math.log(0.25), math.log(1.0))), 0.25, 1.0),
        "owner_list": draw_owner_list(jax.random.fold_in(splits[4], 71), 0),
    }


def lat_cosines(theta_index):
    degree = jnp.arange(DEGREES, dtype=jnp.int32)
    phase_index = (2 * theta_index[:, None] + 1) * degree[None, :] % (4 * NLAT)
    return jnp.cos(phase_index.astype(jnp.float32) * (math.pi / (2 * NLAT))).astype(jnp.bfloat16)

def wave_cosines(wave_ids):
    points = jnp.arange(NLON, dtype=jnp.int32)
    phase_index = wave_ids[:, None] * points[None, :] % NLON
    angles = phase_index.astype(jnp.float32) * (2.0 * math.pi / NLON)
    return jnp.stack([jnp.cos(angles), -jnp.sin(angles)]).astype(jnp.bfloat16)

def radial_slope(values):
    zero_rim = jnp.zeros_like(values[:1])
    upper_side = jnp.concatenate([values[1:], zero_rim], axis=0)
    lower_side = jnp.concatenate([zero_rim, values[:-1]], axis=0)
    return 0.5 * (upper_side - lower_side)

def reference(seed_field, cotangent, step_size, owner_list):
    norm_scale = 2.0 / math.sqrt(DEGREES * WAVES)
    lat_wide = lat_cosines(jnp.arange(NLAT, dtype=jnp.int32)).astype(jnp.float32)
    wave_wide = wave_cosines(owner_list).astype(jnp.float32)
    live_mask = jnp.arange(DEGREES, dtype=jnp.int32)[None, :] >= owner_list[:, None]
    listed = jnp.swapaxes(jnp.take(seed_field, owner_list, axis=4), 3, 4)
    coeffs = jnp.where(live_mask, jnp.concatenate([listed, cotangent], axis=0), jnp.zeros((), jnp.bfloat16))

    def synthesize(radius_block):
        spec_rows = jnp.einsum('csml,tl->csmt', radius_block.astype(jnp.float32), lat_wide).astype(jnp.bfloat16)
        return norm_scale * jnp.einsum('csmt,smf->ctf', spec_rows.astype(jnp.float32), wave_wide)
    grid_field = lax.map(synthesize, jnp.swapaxes(coeffs, 0, 1))
    vel_tor = grid_field[:, 0]
    vel_pol = radial_slope(grid_field[:, 1])
    mag_tor = grid_field[:, 2]
    mag_pol = radial_slope(grid_field[:, 3])
    adj_vel = grid_field[:, 4]
    adj_mag = grid_field[:, 5]
    term_vel = mag_tor * mag_pol - vel_tor * vel_pol
    term_mag = vel_tor * mag_pol - vel_pol * mag_tor
    grad_vtor = -vel_pol * adj_vel + mag_pol * adj_mag
    grad_vpol = -vel_tor * adj_vel - mag_tor * adj_mag
    grad_mtor = mag_pol * adj_vel - vel_pol * adj_mag
    grad_mpol = mag_tor * adj_vel + vel_tor * adj_mag
    back_vpol = -radial_slope(grad_vpol)
    back_mpol = -radial_slope(grad_mpol)
    analysis_in = jnp.stack([term_vel, term_mag, grad_vtor, back_vpol, grad_mtor, back_mpol], axis=1).astype(jnp.bfloat16)
    live_wide = live_mask.astype(jnp.float32)

    def analyse(radius_block):
        back_rows = (norm_scale * jnp.einsum('ctf,smf->csmt', radius_block.astype(jnp.float32), wave_wide)).astype(jnp.bfloat16)
        return jnp.einsum('csmt,tl->csml', back_rows.astype(jnp.float32), lat_wide) * live_wide
    result = jnp.swapaxes(lax.map(analyse, analysis_in), 0, 1)
    nonlinear = result[:2]
    seed_next = listed.astype(jnp.float32) - step_size[0] * result[2:]
    return (nonlinear, seed_next)
```

```python
import functools
import math

import jax
import jax.numpy as jnp
from jax import lax
from jax.experimental import pallas as pl
from jax.experimental.pallas import tpu as pltpu
from jax.sharding import PartitionSpec as P

WAVES = 1024
DEGREES = 1024
NLAT = 1024
NLON = 2048
F_TILE = 256
BF16 = jnp.bfloat16
F32 = jnp.float32


def lat_cosines(theta_index):
    degree = jnp.arange(DEGREES, dtype=jnp.int32)
    phase_index = (2 * theta_index[:, None] + 1) * degree[None, :] % (4 * NLAT)
    return jnp.cos(phase_index.astype(jnp.float32) * (math.pi / (2 * NLAT))).astype(jnp.bfloat16)


def wave_cosines(wave_ids):
    points = jnp.arange(NLON, dtype=jnp.int32)
    phase_index = wave_ids[:, None] * points[None, :] % NLON
    angles = phase_index.astype(jnp.float32) * (2.0 * math.pi / NLON)
    return jnp.stack([jnp.cos(angles), -jnp.sin(angles)]).astype(jnp.bfloat16)


def cos_sin(phase_index, period):
    angles = (phase_index % period).astype(F32) * (2.0 * math.pi / period)
    return jnp.cos(angles), jnp.sin(angles)


def lat_table_of():
    step = 32
    degree = jnp.arange(DEGREES, dtype=jnp.int32)
    coarse = jnp.arange(NLAT // step, dtype=jnp.int32)
    fine = jnp.arange(step, dtype=jnp.int32)
    cos_a, sin_a = cos_sin(2 * step * coarse[:, None] * degree[None, :], 4 * NLAT)
    cos_b, sin_b = cos_sin((2 * fine[:, None] + 1) * degree[None, :], 4 * NLAT)
    table = cos_a[:, None, :] * cos_b[None, :, :] - sin_a[:, None, :] * sin_b[None, :, :]
    return table.astype(BF16).reshape(NLAT, DEGREES)


def wave_table_of(owner_list):
    tiles = jnp.arange(NLON // F_TILE, dtype=jnp.int32)
    fine = jnp.arange(F_TILE, dtype=jnp.int32)
    cos_a, sin_a = cos_sin(F_TILE * tiles[:, None] * owner_list[None, :], NLON)
    cos_b, sin_b = cos_sin(owner_list[:, None] * fine[None, :], NLON)
    cos_a, sin_a = cos_a[:, :, None], sin_a[:, :, None]
    cosine = cos_a * cos_b[None] - sin_a * sin_b[None]
    minus_sine = -sin_a * cos_b[None] - cos_a * sin_b[None]
    table = jnp.stack([cosine.astype(BF16), minus_sine.astype(BF16)], axis=1)
    return table.reshape(NLON // F_TILE, 2 * WAVES, F_TILE)


def estimate(flops, bytes_accessed):
    return pl.CostEstimate(flops=flops, bytes_accessed=bytes_accessed, transcendentals=0)


def permute_kernel(owner_ref, seed_ref, out_ref):
    chans, _, parts, lines, waves = seed_ref.shape
    group, own = out_ref.shape[0], out_ref.shape[4]
    rows = seed_ref[...].reshape(chans * parts * lines, waves)
    wave = lax.broadcasted_iota(jnp.int32, (waves, group * own), 0)
    one_hot = jnp.where(wave == owner_ref[...], 1.0, 0.0).astype(BF16)
    picked = jnp.dot(rows, one_hot, preferred_element_type=F32).astype(BF16)
    for d in range(group):
        part = picked[:, d * own : (d + 1) * own]
        out_ref[d] = part.reshape(chans, parts, lines, own)


def permute(seed_field, owner_list, owners):
    chans, radii, parts, lines, waves = seed_field.shape
    own = waves // owners
    group = 2 if owners % 2 == 0 else 1
    return pl.pallas_call(
        permute_kernel,
        grid=(owners // group,),
        in_specs=[
            pl.BlockSpec((1, group * own), lambda i: (0, i)),
            pl.BlockSpec((chans, radii, parts, lines, waves), lambda i: (0, 0, 0, 0, 0)),
        ],
        out_specs=pl.BlockSpec((group, chans, parts, lines, own), lambda i: (i, 0, 0, 0, 0)),
        out_shape=jax.ShapeDtypeStruct((owners, chans, parts, lines, own), BF16),
        cost_estimate=estimate(2 * chans * parts * lines * waves * waves, 4 * seed_field.size),
        name="permute",
    )(owner_list.reshape(1, waves), seed_field)


def adjoint_rows_kernel(waves_ref, lat_ref, cot_ref, out_ref):
    parts, own, degrees = cot_ref.shape[2:]
    devices, _, _, sub, _ = out_ref.shape
    live = lax.broadcasted_iota(jnp.int32, (own, degrees), 1) >= waves_ref[...]
    for s in range(parts):
        coeffs = jnp.where(live, cot_ref[0, 0, s], jnp.zeros((), BF16))
        rows = lax.dot_general(
            lat_ref[...], coeffs, (((1,), (1,)), ((), ())), preferred_element_type=F32
        )
        out_ref[:, 0, s] = rows.astype(BF16).reshape(devices, sub, own)


def forward_rows_kernel(waves_ref, lat_ref, seed_ref, base_ref, out_ref):
    del base_ref
    owners, _, parts, lines, own = seed_ref.shape
    devices, _, _, sub, _ = out_ref.shape
    degrees = owners * lines
    live = lax.broadcasted_iota(jnp.int32, (degrees, own), 0) >= waves_ref[...]
    coeffs = jnp.concatenate(
        [
            jnp.where(live, seed_ref[:, 0, s].reshape(degrees, own), jnp.zeros((), BF16))
            for s in range(parts)
        ],
        axis=1,
    )
    rows = jnp.dot(lat_ref[...], coeffs, preferred_element_type=F32).astype(BF16)
    for s in range(parts):
        out_ref[:, 0, s] = rows[:, s * own : (s + 1) * own].reshape(devices, sub, own)


def adjoint_rows(my_waves, lat_table, cotangent, seed_chans, devices):
    chans, _, parts, own, degrees = cotangent.shape
    sub = NLAT // devices
    return pl.pallas_call(
        adjoint_rows_kernel,
        grid=(chans,),
        in_specs=[
            pl.BlockSpec((own, 1), lambda c: (0, 0)),
            pl.BlockSpec((NLAT, degrees), lambda c: (0, 0)),
            pl.BlockSpec((1, 1, parts, own, degrees), lambda c: (c, 0, 0, 0, 0)),
        ],
        out_specs=pl.BlockSpec(
            (devices, 1, parts, sub, own), lambda c: (0, seed_chans + c, 0, 0, 0)
        ),
        out_shape=jax.ShapeDtypeStruct((devices, seed_chans + chans, parts, sub, own), BF16),
        cost_estimate=estimate(2 * cotangent.size * NLAT, 4 * cotangent.size + 2 * lat_table.size),
        name="adjoint_rows",
    )(my_waves.reshape(own, 1), lat_table, cotangent)


def forward_rows(my_waves, lat_table, owned_seed, base):
    owners, chans, parts, lines, own = owned_seed.shape
    devices, _, _, sub, _ = base.shape
    return pl.pallas_call(
        forward_rows_kernel,
        grid=(chans,),
        in_specs=[
            pl.BlockSpec((1, own), lambda c: (0, 0)),
            pl.BlockSpec((NLAT, owners * lines), lambda c: (0, 0)),
            pl.BlockSpec((owners, 1, parts, lines, own), lambda c: (0, c, 0, 0, 0)),
            pl.BlockSpec(memory_space=pl.ANY),
        ],
        out_specs=pl.BlockSpec((devices, 1, parts, sub, own), lambda c: (0, c, 0, 0, 0)),
        out_shape=jax.ShapeDtypeStruct(base.shape, BF16),
        input_output_aliases={3: 0},
        cost_estimate=estimate(2 * owned_seed.size * NLAT, 4 * owned_seed.size + 2 * lat_table.size),
        name="forward_rows",
    )(my_waves.reshape(1, own), lat_table, owned_seed, base)


def slope(values):
    rim = jnp.zeros_like(values[:1])
    upper = jnp.concatenate([values[1:], rim], axis=0)
    lower = jnp.concatenate([rim, values[:-1]], axis=0)
    return 0.5 * (upper - lower)


def grid_kernel(f_tiles, norm_scale, got_ref, tab_ref, back_tab_ref, out_ref, rows_ref, terms_ref):
    step = pl.program_id(0)
    devices, chans, parts, sub, own = got_ref.shape
    radii = rows_ref.shape[1]
    owners = devices // radii
    rows = chans * radii * sub
    group = out_ref.shape[0] // radii

    @pl.when(step == 0)
    def _():
        for s in range(parts):
            for d in range(owners):
                start = (s * owners + d) * own
                for r in range(radii):
                    rows_ref[:, r, :, start : start + own] = got_ref[d * radii + r, :, s]

    @pl.when(step < f_tiles)
    def _():
        field = norm_scale * jnp.dot(
            rows_ref[...].reshape(rows, -1), tab_ref[0], preferred_element_type=F32
        )
        field = field.reshape(chans, radii, sub, F_TILE)
        vel_tor = field[0]
        vel_pol = slope(field[1])
        mag_tor = field[2]
        mag_pol = slope(field[3])
        adj_vel = field[4]
        adj_mag = field[5]
        grad_vpol = -vel_tor * adj_vel - mag_tor * adj_mag
        grad_mpol = mag_tor * adj_vel + vel_tor * adj_mag
        terms = [
            mag_tor * mag_pol - vel_tor * vel_pol,
            vel_tor * mag_pol - vel_pol * mag_tor,
            -vel_pol * adj_vel + mag_pol * adj_mag,
            -slope(grad_vpol),
            mag_pol * adj_vel - vel_pol * adj_mag,
            -slope(grad_mpol),
        ]
        for c, term in enumerate(terms):
            terms_ref[step, c] = term.astype(BF16)

    @pl.when(step >= f_tiles)
    def _():
        total = None
        for a in range(f_tiles):
            part = lax.dot_general(
                terms_ref[a].reshape(rows, F_TILE),
                back_tab_ref[a],
                (((1,), (1,)), ((), ())),
                preferred_element_type=F32,
            )
            total = part if total is None else total + part
        back = (norm_scale * total).astype(BF16).reshape(chans, radii, sub, group * own)
        for d in range(group):
            for r in range(radii):
                out_ref[d * radii + r, :, 0] = back[:, r, :, d * own : (d + 1) * own]


def grid_step(got, table, radii):
    devices, chans, parts, sub, own = got.shape
    owners = devices // radii
    f_tiles, waves_wide, _ = table.shape
    group = 2 if owners % 2 == 0 else 1
    per_part = owners // group
    norm_scale = 2.0 / math.sqrt(DEGREES * WAVES)

    def back(i):
        return jnp.maximum(i - f_tiles, 0)

    return pl.pallas_call(
        functools.partial(grid_kernel, f_tiles, norm_scale),
        grid=(f_tiles + parts * per_part,),
        in_specs=[
            pl.BlockSpec(got.shape, lambda i: (0, 0, 0, 0, 0)),
            pl.BlockSpec((1, waves_wide, F_TILE), lambda i: (jnp.minimum(i, f_tiles - 1), 0, 0)),
            pl.BlockSpec((f_tiles, group * own, F_TILE), lambda i: (0, back(i), 0)),
        ],
        out_specs=pl.BlockSpec(
            (group * radii, chans, 1, sub, own),
            lambda i: (back(i) % per_part, 0, back(i) // per_part, 0, 0),
        ),
        out_shape=jax.ShapeDtypeStruct(got.shape, BF16),
        scratch_shapes=[
            pltpu.VMEM((chans, radii, sub, waves_wide), BF16),
            pltpu.VMEM((f_tiles, chans, radii, sub, F_TILE), BF16),
        ],
        cost_estimate=estimate(
            4 * chans * radii * sub * waves_wide * NLON, 4 * got.size + 4 * table.size
        ),
        name="grid_step",
    )(got, table, table)


def result_kernel(pair, step_ref, waves_ref, lat_ref, back_ref, listed_ref, non_ref, next_ref):
    block = pl.program_id(0)
    devices, _, parts, sub, own = back_ref.shape
    degrees = lat_ref.shape[1]
    live = lax.broadcasted_iota(jnp.int32, (own, degrees), 1) >= waves_ref[...]
    columns = jnp.concatenate(
        [
            back_ref[:, c, s].reshape(devices * sub, own)
            for c in range(pair)
            for s in range(parts)
        ],
        axis=1,
    )
    result = lax.dot_general(
        columns, lat_ref[...], (((0,), (0,)), ((), ())), preferred_element_type=F32
    )
    for c in range(pair):
        for s in range(parts):
            start = (c * parts + s) * own
            value = jnp.where(live, result[start : start + own], 0.0)

            @pl.when(block == 0)
            def _(value=value, c=c, s=s):
                non_ref[c, 0, s] = value

            @pl.when(block > 0)
            def _(value=value, c=c, s=s):
                next_ref[c, 0, s] = listed_ref[c, s].astype(F32) - step_ref[0] * value


def results(step_size, my_waves, lat_table, returned, listed):
    devices, chans, parts, sub, own = returned.shape
    degrees = lat_table.shape[1]
    pair = 2
    seed_chans = listed.shape[0]

    def seed_block(i):
        return jnp.maximum(i - 1, 0)

    return pl.pallas_call(
        functools.partial(result_kernel, pair),
        grid=(chans // pair,),
        in_specs=[
            pl.BlockSpec(memory_space=pltpu.SMEM),
            pl.BlockSpec((own, 1), lambda i: (0, 0)),
            pl.BlockSpec(lat_table.shape, lambda i: (0, 0)),
            pl.BlockSpec((devices, pair, parts, sub, own), lambda i: (0, i, 0, 0, 0)),
            pl.BlockSpec((pair, parts, own, degrees), lambda i: (seed_block(i), 0, 0, 0)),
        ],
        out_specs=[
            pl.BlockSpec((pair, 1, parts, own, degrees), lambda i: (0, 0, 0, 0, 0)),
            pl.BlockSpec((pair, 1, parts, own, degrees), lambda i: (seed_block(i), 0, 0, 0, 0)),
        ],
        out_shape=[
            jax.ShapeDtypeStruct((chans - seed_chans, 1, parts, own, degrees), F32),
            jax.ShapeDtypeStruct((seed_chans, 1, parts, own, degrees), F32),
        ],
        cost_estimate=estimate(2 * returned.size * degrees, 2 * returned.size + 4 * returned.size),
        name="results",
    )(step_size, my_waves.reshape(own, 1), lat_table, returned, listed)


def local(seed_field, cotangent, step_size, owner_list):
    owners, radii = lax.axis_size("ma"), lax.axis_size("row")
    own = cotangent.shape[3]
    my_waves = lax.dynamic_slice_in_dim(owner_list, lax.axis_index("ma") * own, own)
    permuted = permute(seed_field, owner_list, owners)
    owned_seed = lax.all_to_all(permuted, "ma", 0, 0, tiled=True)
    lat_table = lat_table_of()
    wave_table = wave_table_of(owner_list)
    base = adjoint_rows(my_waves, lat_table, cotangent, seed_field.shape[0], owners * radii)
    spec_rows = forward_rows(my_waves, lat_table, owned_seed, base)
    gridded = lax.all_to_all(spec_rows, ("ma", "row"), 0, 0, tiled=True)
    listed = jnp.transpose(owned_seed, (1, 2, 4, 0, 3))
    listed = listed.reshape(listed.shape[:3] + (DEGREES,))
    back_rows = grid_step(gridded, wave_table, radii)
    returned = lax.all_to_all(back_rows, ("ma", "row"), 0, 0, tiled=True)
    nonlinear, seed_next = results(step_size, my_waves, lat_table, returned, listed)
    return (nonlinear, seed_next)


def local_small(seed_field, cotangent, step_size, owner_list):
    owner_count = lax.axis_size("ma")
    own_waves = cotangent.shape[3]
    norm_scale = 2.0 / math.sqrt(DEGREES * WAVES)
    block_width = min(128, WAVES)
    my_waves = lax.dynamic_slice_in_dim(owner_list, lax.axis_index("ma") * own_waves, own_waves)
    degree = jnp.arange(DEGREES, dtype=jnp.int32)
    live_cols = degree[:, None] >= my_waves[None, :]
    live_rows = jnp.transpose(live_cols)
    zero_value = jnp.zeros((), jnp.bfloat16)
    listed = jnp.take(seed_field, owner_list, axis=4)
    owned_seed = lax.all_to_all(listed, "ma", split_axis=4, concat_axis=3, tiled=True)
    lat_table = lat_cosines(jnp.arange(NLAT, dtype=jnp.int32))
    forward_rows = jnp.einsum(
        "crslk,tl->crstk",
        jnp.where(live_cols, owned_seed, zero_value),
        lat_table,
        preferred_element_type=jnp.float32,
    )
    adjoint_rows = jnp.einsum(
        "crskl,tl->crstk",
        jnp.where(live_rows, cotangent, zero_value),
        lat_table,
        preferred_element_type=jnp.float32,
    )
    spec_rows = jnp.concatenate([forward_rows, adjoint_rows], axis=0).astype(jnp.bfloat16)
    gridded = lax.all_to_all(
        lax.all_to_all(spec_rows, "ma", split_axis=3, concat_axis=4, tiled=True),
        "row",
        split_axis=3,
        concat_axis=1,
        tiled=True,
    )
    grid_field = None
    for start in range(0, WAVES, block_width):
        wave_block = wave_cosines(owner_list[start : start + block_width])
        partial_grid = jnp.einsum(
            "crsjm,smf->crjf",
            gridded[..., start : start + block_width],
            wave_block,
            preferred_element_type=jnp.float32,
        )
        grid_field = partial_grid if grid_field is None else grid_field + partial_grid
    grid_field = norm_scale * grid_field
    radial_pair = jnp.stack([grid_field[1], grid_field[3]])
    padded = jnp.pad(radial_pair, ((0, 0), (1, 1), (0, 0), (0, 0)))
    slopes = 0.5 * (padded[:, 2:] - padded[:, :-2])
    vel_tor = grid_field[0]
    mag_tor = grid_field[2]
    adj_vel = grid_field[4]
    adj_mag = grid_field[5]
    vel_pol = slopes[0]
    mag_pol = slopes[1]
    term_vel = mag_tor * mag_pol - vel_tor * vel_pol
    term_mag = vel_tor * mag_pol - vel_pol * mag_tor
    grad_vtor = -vel_pol * adj_vel + mag_pol * adj_mag
    grad_vpol = -vel_tor * adj_vel - mag_tor * adj_mag
    grad_mtor = mag_pol * adj_vel - vel_pol * adj_mag
    grad_mpol = mag_tor * adj_vel + vel_tor * adj_mag
    cotangent_pair = jnp.stack([grad_vpol, grad_mpol])
    padded_back = jnp.pad(cotangent_pair, ((0, 0), (1, 1), (0, 0), (0, 0)))
    back_slopes = 0.5 * (padded_back[:, :-2] - padded_back[:, 2:])
    analysis_in = jnp.stack(
        [term_vel, term_mag, grad_vtor, back_slopes[0], grad_mtor, back_slopes[1]]
    ).astype(jnp.bfloat16)
    spectra_parts = []
    for start in range(0, WAVES, block_width):
        wave_block = wave_cosines(owner_list[start : start + block_width])
        spectra_parts.append(
            jnp.einsum(
                "crjf,smf->crsjm", analysis_in, wave_block, preferred_element_type=jnp.float32
            )
        )
    spectra = (norm_scale * jnp.concatenate(spectra_parts, axis=4)).astype(jnp.bfloat16)
    position = jnp.arange(NLAT, dtype=jnp.int32)
    returned = lax.all_to_all(
        lax.all_to_all(spectra, "ma", split_axis=4, concat_axis=3, tiled=True),
        "row",
        split_axis=1,
        concat_axis=3,
        tiled=True,
    )
    sub_rows = spectra.shape[3]
    radial_part = position // (owner_count * sub_rows)
    owner_part = position // sub_rows % owner_count
    theta_index = owner_part * (NLAT // owner_count) + radial_part * sub_rows + position % sub_rows
    back_table = lat_cosines(theta_index)
    result = jnp.einsum("crstk,tl->crskl", returned, back_table, preferred_element_type=jnp.float32)
    result = jnp.where(live_rows, result, 0.0)
    nonlinear = result[:2]
    seed_next = jnp.swapaxes(owned_seed, 3, 4).astype(jnp.float32) - step_size[0] * result[2:]
    return (nonlinear, seed_next)


def fits(mesh):
    owners, radii = mesh.shape["ma"], mesh.shape["row"]
    own, sub = WAVES // owners, NLAT // (owners * radii)
    return own % 128 == 0 and sub % 16 == 0


def solution(mesh):
    return jax.shard_map(
        local if fits(mesh) else local_small,
        mesh=mesh,
        in_specs=(P(None, "row", None, "ma", None), P(None, "row", None, "ma", None), P(), P()),
        out_specs=(P(None, "row", None, "ma", None), P(None, "row", None, "ma", None)),
        check_vma=False,
    )
```

```python
import functools
import math

import jax
import jax.numpy as jnp
from jax import lax
from jax.experimental import pallas as pl
from jax.experimental.pallas import tpu as pltpu
from jax.sharding import PartitionSpec as P

WAVES = 1024
DEGREES = 1024
NLAT = 1024
NLON = 2048
F_TILE = 256
BF16 = jnp.bfloat16
F32 = jnp.float32


def lat_cosines(theta_index):
    degree = jnp.arange(DEGREES, dtype=jnp.int32)
    phase_index = (2 * theta_index[:, None] + 1) * degree[None, :] % (4 * NLAT)
    return jnp.cos(phase_index.astype(jnp.float32) * (math.pi / (2 * NLAT))).astype(jnp.bfloat16)


def wave_cosines(wave_ids):
    points = jnp.arange(NLON, dtype=jnp.int32)
    phase_index = wave_ids[:, None] * points[None, :] % NLON
    angles = phase_index.astype(jnp.float32) * (2.0 * math.pi / NLON)
    return jnp.stack([jnp.cos(angles), -jnp.sin(angles)]).astype(jnp.bfloat16)


def cos_sin(phase_index, period):
    angles = (phase_index % period).astype(F32) * (2.0 * math.pi / period)
    return jnp.cos(angles), jnp.sin(angles)


def lat_table_of(coarse, degree, step):
    fine = jnp.arange(step, dtype=jnp.int32)
    cos_a, sin_a = cos_sin(2 * step * coarse[:, None] * degree[None, :], 4 * NLAT)
    cos_b, sin_b = cos_sin((2 * fine[:, None] + 1) * degree[None, :], 4 * NLAT)
    table = cos_a[:, None, :] * cos_b[None, :, :] - sin_a[:, None, :] * sin_b[None, :, :]
    return table.astype(BF16).reshape(coarse.shape[0] * step, degree.shape[0])


def wave_tables_of(waves):
    tiles = jnp.arange(NLON // F_TILE, dtype=jnp.int32)
    fine = jnp.arange(F_TILE, dtype=jnp.int32)
    cos_a, sin_a = cos_sin(F_TILE * tiles[:, None] * waves[None, :], NLON)
    cos_b, sin_b = cos_sin(waves[:, None] * fine[None, :], NLON)
    cos_a, sin_a = cos_a[:, :, None], sin_a[:, :, None]
    cosine = cos_a * cos_b[None] - sin_a * sin_b[None]
    minus_sine = -sin_a * cos_b[None] - cos_a * sin_b[None]
    return cosine.astype(BF16), minus_sine.astype(BF16)


def estimate(flops, bytes_accessed):
    return pl.CostEstimate(flops=int(flops), bytes_accessed=int(bytes_accessed), transcendentals=0)


def whole(shape):
    return pl.BlockSpec(shape, lambda *_: (0,) * len(shape))


def permute_kernel(owner_ref, seed_ref, *out_refs):
    chans, _, parts, lines, waves = seed_ref.shape
    own = out_refs[0].shape[-1]
    me = lax.axis_index("ma")
    rows = seed_ref[...].reshape(chans * parts * lines, waves)
    wave = lax.broadcasted_iota(jnp.int32, (waves, 2 * own), 0)
    for k in reversed(range(0, len(out_refs), 2)):
        wanted = jnp.concatenate(
            [owner_ref[pl.ds(me ^ k, 1), :], owner_ref[pl.ds(me ^ (k + 1), 1), :]], axis=1
        )
        one_hot = jnp.where(wave == wanted, 1.0, 0.0).astype(BF16)
        picked = jnp.dot(rows, one_hot, preferred_element_type=F32).astype(BF16)
        for d in range(2):
            part = picked[:, d * own : (d + 1) * own]
            out_refs[k + d][...] = part.reshape(chans, parts, lines, own)


def permute(seed_field, owner_list, owners):
    chans, _, parts, lines, waves = seed_field.shape
    own = waves // owners
    slot = jax.ShapeDtypeStruct((chans, parts, lines, own), BF16)
    return pl.pallas_call(
        permute_kernel,
        out_shape=[slot] * owners,
        cost_estimate=estimate(2 * seed_field.size * waves, 4 * seed_field.size),
        name="permute",
    )(owner_list.reshape(owners, own), seed_field)


def adjoint_kernel(waves_ref, lat_ref, cot_ref, *out_refs):
    parts, own, degrees = cot_ref.shape[2:]
    sub = out_refs[0].shape[2]
    live = lax.broadcasted_iota(jnp.int32, (own, degrees), 1) >= waves_ref[...]
    for s in range(parts):
        coeffs = jnp.where(live, cot_ref[0, 0, s], jnp.zeros((), BF16))
        rows = lax.dot_general(
            lat_ref[...], coeffs, (((1,), (1,)), ((), ())), preferred_element_type=F32
        ).astype(BF16)
        for k, out_ref in enumerate(out_refs):
            out_ref[0, s] = rows[k * sub : (k + 1) * sub]


def adjoint_rows(my_waves, lat_table, cotangent, owners):
    chans, _, parts, own, degrees = cotangent.shape
    sub = NLAT // owners
    return pl.pallas_call(
        adjoint_kernel,
        grid=(chans,),
        in_specs=[
            whole((own, 1)),
            whole(lat_table.shape),
            pl.BlockSpec((1, 1, parts, own, degrees), lambda c: (c, 0, 0, 0, 0)),
        ],
        out_specs=[pl.BlockSpec((1, parts, sub, own), lambda c: (c, 0, 0, 0))] * owners,
        out_shape=[jax.ShapeDtypeStruct((chans, parts, sub, own), BF16)] * owners,
        cost_estimate=estimate(2 * cotangent.size * NLAT, 4 * cotangent.size + 2 * lat_table.size),
        name="adjoint_rows",
    )(my_waves.reshape(own, 1), lat_table, cotangent)


def forward_kernel(owners, joined, waves_ref, lat_ref, *refs):
    seed_refs, out_refs = refs[:owners], refs[owners:]
    _, parts, lines, own = seed_refs[0].shape
    sub = lat_ref.shape[0] // owners
    me = lax.axis_index("ma")
    line = lax.broadcasted_iota(jnp.int32, (lines, own), 0)
    live = [line + (me ^ k) * lines >= waves_ref[...] for k in range(owners)]
    coeffs = jnp.concatenate(
        [
            jnp.concatenate(
                [
                    jnp.where(live[k], seed_refs[k][0, s], jnp.zeros((), BF16))
                    for k in range(owners)
                ],
                axis=0,
            )
            for s in range(parts)
        ],
        axis=1,
    )
    rows = jnp.dot(lat_ref[...], coeffs, preferred_element_type=F32).astype(BF16)
    for k in range(owners):
        for s in range(parts):
            part = rows[k * sub : (k + 1) * sub, s * own : (s + 1) * own]
            if joined:
                out_refs[0][k, 0, s] = part
            else:
                out_refs[k][0, s] = part


def forward_rows(my_waves, lat_table, owned_seed, first, joined):
    owners = len(owned_seed)
    chans, parts, lines, own = owned_seed[0].shape
    picked = chans // 2
    sub = lat_table.shape[0] // owners
    if joined:
        out_specs = [pl.BlockSpec((owners, 1, parts, sub, own), lambda c: (0, c, 0, 0, 0))]
        out_shape = [jax.ShapeDtypeStruct((owners, picked, parts, sub, own), BF16)]
    else:
        out_specs = [pl.BlockSpec((1, parts, sub, own), lambda c: (c, 0, 0, 0))] * owners
        out_shape = [jax.ShapeDtypeStruct((picked, parts, sub, own), BF16)] * owners
    size = owners * owned_seed[0].size // 2
    return pl.pallas_call(
        functools.partial(forward_kernel, owners, joined),
        grid=(picked,),
        in_specs=[whole((1, own)), whole(lat_table.shape)]
        + [pl.BlockSpec((1, parts, lines, own), lambda c: (2 * c + first, 0, 0, 0))] * owners,
        out_specs=out_specs,
        out_shape=out_shape,
        cost_estimate=estimate(2 * size * NLAT, 4 * size + 2 * lat_table.size),
        name="forward_rows",
    )(my_waves.reshape(1, own), lat_table, *owned_seed)


def slope_kernel(plus_ref, minus_ref, *out_refs):
    for k, out_ref in enumerate(out_refs):
        out_ref[...] = (0.5 * (plus_ref[k].astype(F32) - minus_ref[k].astype(F32))).astype(BF16)


def slope_rows(plus, minus):
    owners = plus.shape[0]
    return pl.pallas_call(
        slope_kernel,
        out_shape=[jax.ShapeDtypeStruct(plus.shape[1:], BF16)] * owners,
        cost_estimate=estimate(4 * plus.size, 6 * plus.size),
        name="slope_rows",
    )(plus, minus)


def gather_rows(rows_ref, start, slots):
    chans, parts, _, own = slots[0].shape
    for s in range(parts):
        for k, slot in enumerate(slots):
            column = (s * len(slots) + k) * own
            for c in range(chans):
                rows_ref[start + c, :, column : column + own] = slot[c, s]


def synthesis(norm_scale, rows_ref, cos_ref, sin_ref):
    chans, sub, wide = rows_ref.shape
    rows = rows_ref[...].reshape(chans * sub, wide)
    half = wide // 2
    field = jnp.dot(rows[:, :half], cos_ref[0], preferred_element_type=F32)
    field += jnp.dot(rows[:, half:], sin_ref[0], preferred_element_type=F32)
    return (norm_scale * field).reshape(chans, sub, F_TILE)


def field_kernel(owners, norm_scale, cos_ref, sin_ref, *refs):
    tor_refs, adj_refs = refs[:owners], refs[owners : 2 * owners]
    out_ref, rows_ref = refs[2 * owners :]

    @pl.when(pl.program_id(0) == 0)
    def _():
        gather_rows(rows_ref, 0, tor_refs)
        gather_rows(rows_ref, tor_refs[0].shape[0], adj_refs)

    out_ref[0] = synthesis(norm_scale, rows_ref, cos_ref, sin_ref)


def fields(norm_scale, cosine, minus_sine, tor, adj):
    owners = len(tor)
    chans, parts, sub, own = tor[0].shape
    f_tiles, waves, _ = cosine.shape
    table = pl.BlockSpec((1, waves, F_TILE), lambda i: (i, 0, 0))
    return pl.pallas_call(
        functools.partial(field_kernel, owners, norm_scale),
        grid=(f_tiles,),
        in_specs=[table, table] + [whole(tor[0].shape)] * (2 * owners),
        out_specs=pl.BlockSpec((1, 2 * chans, sub, F_TILE), lambda i: (i, 0, 0, 0)),
        out_shape=jax.ShapeDtypeStruct((f_tiles, 2 * chans, sub, F_TILE), F32),
        scratch_shapes=[pltpu.VMEM((2 * chans, sub, parts * waves), BF16)],
        cost_estimate=estimate(8 * chans * sub * waves * NLON, 4 * cosine.size),
        name="fields",
    )(cosine, minus_sine, *tor, *adj)


def terms_kernel(owners, norm_scale, cos_ref, sin_ref, field_ref, *refs):
    pol_refs = refs[:owners]
    out_ref, rows_ref = refs[owners:]

    @pl.when(pl.program_id(0) == 0)
    def _():
        gather_rows(rows_ref, 0, pol_refs)

    slope = synthesis(norm_scale, rows_ref, cos_ref, sin_ref)
    vel_pol, mag_pol = slope[0], slope[1]
    vel_tor, mag_tor = field_ref[0, 0], field_ref[0, 1]
    adj_vel, adj_mag = field_ref[0, 2], field_ref[0, 3]
    terms = [
        mag_tor * mag_pol - vel_tor * vel_pol,
        vel_tor * mag_pol - vel_pol * mag_tor,
        -vel_pol * adj_vel + mag_pol * adj_mag,
        mag_pol * adj_vel - vel_pol * adj_mag,
        -vel_tor * adj_vel - mag_tor * adj_mag,
        mag_tor * adj_vel + vel_tor * adj_mag,
    ]
    for c, term in enumerate(terms):
        out_ref[0, c] = term.astype(BF16)


def grid_terms(norm_scale, cosine, minus_sine, field, pol):
    owners = len(pol)
    chans, parts, sub, own = pol[0].shape
    f_tiles, waves, _ = cosine.shape
    table = pl.BlockSpec((1, waves, F_TILE), lambda i: (i, 0, 0))
    return pl.pallas_call(
        functools.partial(terms_kernel, owners, norm_scale),
        grid=(f_tiles,),
        in_specs=[table, table, pl.BlockSpec((1,) + field.shape[1:], lambda i: (i, 0, 0, 0))]
        + [whole(pol[0].shape)] * owners,
        out_specs=pl.BlockSpec((1, 3 * chans, sub, F_TILE), lambda i: (i, 0, 0, 0)),
        out_shape=jax.ShapeDtypeStruct((f_tiles, 3 * chans, sub, F_TILE), BF16),
        scratch_shapes=[pltpu.VMEM((chans, sub, parts * waves), BF16)],
        cost_estimate=estimate(4 * chans * sub * waves * NLON, 4 * cosine.size + 4 * field.size),
        name="grid_terms",
    )(cosine, minus_sine, field, *pol)


def back_kernel(joined, norm_scale, terms_ref, cos_ref, sin_ref, *out_refs):
    step = pl.program_id(0)
    f_tiles, chans, sub, _ = terms_ref.shape
    own = cos_ref.shape[1] // 2
    for s, table_ref in enumerate((cos_ref, sin_ref)):
        total = None
        for a in range(f_tiles):
            part = lax.dot_general(
                terms_ref[a].reshape(chans * sub, F_TILE),
                table_ref[a],
                (((1,), (1,)), ((), ())),
                preferred_element_type=F32,
            )
            total = part if total is None else total + part
        back = (norm_scale * total).astype(BF16).reshape(chans, sub, 2 * own)
        for d in range(2):
            part = back[:, :, d * own : (d + 1) * own]
            if joined:
                out_refs[0][d, :, s] = part
                continue
            for k in range(d, len(out_refs), 2):

                @pl.when(step == k // 2)
                def _(part=part, k=k, s=s):
                    out_refs[k][:, s] = part


def back_rows(norm_scale, terms, cosine, minus_sine, chans, block, slots, joined):
    f_tiles, _, sub, _ = terms.shape
    waves = cosine.shape[1]
    own = waves // lax.axis_size("ma")
    first, count = slots
    table = pl.BlockSpec((f_tiles, 2 * own, F_TILE), lambda i: (0, first // 2 + i, 0))
    if joined:
        out_specs = [pl.BlockSpec((2, chans, 2, sub, own), lambda i: (i, 0, 0, 0, 0))]
        out_shape = [jax.ShapeDtypeStruct((count, chans, 2, sub, own), BF16)]
    else:
        out_specs = [whole((chans, 2, sub, own))] * count
        out_shape = [jax.ShapeDtypeStruct((chans, 2, sub, own), BF16)] * count
    return pl.pallas_call(
        functools.partial(back_kernel, joined, norm_scale),
        grid=(count // 2,),
        in_specs=[
            pl.BlockSpec((f_tiles, chans, sub, F_TILE), lambda i: (0, block, 0, 0)),
            table,
            table,
        ],
        out_specs=out_specs,
        out_shape=out_shape,
        cost_estimate=estimate(
            4 * chans * sub * NLON * own * count, 2 * terms.size + 4 * cosine.size
        ),
        name="back_rows",
    )(terms, cosine, minus_sine)


def listed_kernel(*refs):
    owners = len(refs) - 1
    out_ref = refs[owners]
    _, parts, lines, own = refs[0].shape
    me = lax.axis_index("ma")
    for k in range(owners):
        column = pl.multiple_of((me ^ k) * lines, lines)
        for s in range(parts):
            out_ref[0, s, :, pl.ds(column, lines)] = refs[k][0, s].astype(F32).T.astype(BF16)


def list_seed(owned_seed):
    owners = len(owned_seed)
    chans, parts, lines, own = owned_seed[0].shape
    return pl.pallas_call(
        listed_kernel,
        grid=(chans,),
        in_specs=[pl.BlockSpec((1, parts, lines, own), lambda c: (c, 0, 0, 0))] * owners,
        out_specs=pl.BlockSpec((1, parts, own, owners * lines), lambda c: (c, 0, 0, 0)),
        out_shape=jax.ShapeDtypeStruct((chans, parts, own, owners * lines), BF16),
        cost_estimate=estimate(0, 4 * owners * owned_seed[0].size),
        name="list_seed",
    )(*owned_seed)


def analysed(owners, waves_ref, lat_ref, slots):
    _, parts, sub, own = slots[0].shape
    columns = jnp.concatenate(
        [
            jnp.concatenate([slots[k][0, s] for k in range(owners)], axis=0)
            for s in range(parts)
        ],
        axis=1,
    )
    result = lax.dot_general(
        columns, lat_ref[...], (((0,), (0,)), ((), ())), preferred_element_type=F32
    )
    degrees = lat_ref.shape[1]
    live = lax.broadcasted_iota(jnp.int32, (own, degrees), 1) >= waves_ref[...]
    return [jnp.where(live, result[s * own : (s + 1) * own], 0.0) for s in range(parts)]


def other_kernel(owners, step_ref, waves_ref, lat_ref, listed_ref, *refs):
    slots = refs[:owners]
    non_ref, next_ref = refs[owners:]
    chan = pl.program_id(0)
    values = analysed(owners, waves_ref, lat_ref, slots)

    @pl.when(chan < 2)
    def _():
        for s, value in enumerate(values):
            non_ref[0, 0, s] = value

    @pl.when(chan >= 2)
    def _():
        for s, value in enumerate(values):
            next_ref[0, 0, s] = listed_ref[0, s].astype(F32) - step_ref[0] * value


def other_results(step_size, my_waves, lat_table, listed, slots):
    owners = len(slots)
    chans, parts, sub, own = slots[0].shape
    degrees = lat_table.shape[1]

    def tor(c):
        return 2 * jnp.maximum(c - 2, 0)

    return pl.pallas_call(
        functools.partial(other_kernel, owners),
        grid=(chans,),
        in_specs=[
            pl.BlockSpec(memory_space=pltpu.SMEM),
            whole((own, 1)),
            whole(lat_table.shape),
            pl.BlockSpec((1, parts, own, degrees), lambda c: (tor(c), 0, 0, 0)),
        ]
        + [pl.BlockSpec((1, parts, sub, own), lambda c: (c, 0, 0, 0))] * owners,
        out_specs=[
            pl.BlockSpec((1, 1, parts, own, degrees), lambda c: (jnp.minimum(c, 1), 0, 0, 0, 0)),
            pl.BlockSpec((1, 1, parts, own, degrees), lambda c: (tor(c), 0, 0, 0, 0)),
        ],
        out_shape=[
            jax.ShapeDtypeStruct((2, 1, parts, own, degrees), F32),
            jax.ShapeDtypeStruct((4, 1, parts, own, degrees), F32),
        ],
        cost_estimate=estimate(
            2 * chans * parts * own * NLAT * degrees, 6 * chans * parts * own * degrees
        ),
        name="other_results",
    )(step_size, my_waves.reshape(own, 1), lat_table, listed, *slots)


def slope_result_kernel(owners, step_ref, waves_ref, lat_ref, listed_ref, base_ref, *refs):
    del base_ref
    next_ref = refs[owners]
    for s, value in enumerate(analysed(owners, waves_ref, lat_ref, refs[:owners])):
        next_ref[0, 0, s] = listed_ref[0, s].astype(F32) - step_ref[0] * value


def slope_results(step_size, my_waves, lat_table, listed, base, slots):
    owners = len(slots)
    chans, parts, sub, own = slots[0].shape
    degrees = lat_table.shape[1]
    return pl.pallas_call(
        functools.partial(slope_result_kernel, owners),
        grid=(chans,),
        in_specs=[
            pl.BlockSpec(memory_space=pltpu.SMEM),
            whole((own, 1)),
            whole(lat_table.shape),
            pl.BlockSpec((1, parts, own, degrees), lambda c: (2 * c + 1, 0, 0, 0)),
            pl.BlockSpec(memory_space=pl.ANY),
        ]
        + [pl.BlockSpec((1, parts, sub, own), lambda c: (c, 0, 0, 0))] * owners,
        out_specs=pl.BlockSpec((1, 1, parts, own, degrees), lambda c: (2 * c + 1, 0, 0, 0, 0)),
        out_shape=jax.ShapeDtypeStruct(base.shape, F32),
        input_output_aliases={4: 0},
        cost_estimate=estimate(
            2 * chans * parts * own * NLAT * degrees, 6 * chans * parts * own * degrees
        ),
        name="slope_results",
    )(step_size, my_waves.reshape(own, 1), lat_table, listed, base, *slots)


def exchange(slots):
    owners = len(slots)
    got = list(slots)
    for k in reversed(range(1, owners)):
        got[k] = lax.ppermute(slots[k], "ma", [(i, i ^ k) for i in range(owners)])
    return got


def neighbours(values):
    radii = lax.axis_size("row")
    above = lax.ppermute(values, "row", [(r, r - 1) for r in range(1, radii)])
    below = lax.ppermute(values, "row", [(r, r + 1) for r in range(radii - 1)])
    return above, below


def local(seed_field, cotangent, step_size, owner_list):
    owners = lax.axis_size("ma")
    own = cotangent.shape[3]
    norm_scale = 2.0 / math.sqrt(DEGREES * WAVES)
    me = lax.axis_index("ma")
    my_waves = lax.dynamic_slice_in_dim(owner_list, me * own, own)
    slot_ids = me ^ jnp.arange(owners, dtype=jnp.int32)
    owned_seed = exchange(permute(seed_field, owner_list, owners))
    sub, lines = NLAT // owners, DEGREES // owners
    step = 32
    parts_of = jnp.arange(sub // step, dtype=jnp.int32)
    coarse = (slot_ids[:, None] * (sub // step) + parts_of[None, :]).reshape(-1)
    degree = jnp.arange(DEGREES, dtype=jnp.int32)
    lines_of = jnp.arange(lines, dtype=jnp.int32)
    slot_degree = (slot_ids[:, None] * lines + lines_of[None, :]).reshape(-1)
    lat_plain = lat_table_of(coarse, degree, step)
    lat_slots = lat_table_of(coarse, slot_degree, step)
    slot_waves = jnp.take(owner_list.reshape(owners, own), slot_ids, axis=0).reshape(-1)
    cosine, minus_sine = wave_tables_of(slot_waves)
    adj = exchange(adjoint_rows(my_waves, lat_plain, cotangent, owners))
    (pol_rows,) = forward_rows(my_waves, lat_slots, owned_seed, 1, True)
    above, below = neighbours(pol_rows)
    tor = exchange(forward_rows(my_waves, lat_slots, owned_seed, 0, False))
    listed = list_seed(owned_seed)
    pol = exchange(slope_rows(above, below))
    field = fields(norm_scale, cosine, minus_sine, tor, adj)
    terms = grid_terms(norm_scale, cosine, minus_sine, field, pol)
    half = owners // 2
    (raw,) = back_rows(norm_scale, terms, cosine, minus_sine, 2, 2, (0, owners), True)
    far = back_rows(norm_scale, terms, cosine, minus_sine, 4, 0, (half, half), False)
    near = back_rows(norm_scale, terms, cosine, minus_sine, 4, 0, (0, half), False)
    raw_above, raw_below = neighbours(raw)
    others = exchange(list(near) + list(far))
    back_pol = exchange(slope_rows(raw_below, raw_above))
    nonlinear, base = other_results(step_size, my_waves, lat_plain, listed, others)
    seed_next = slope_results(step_size, my_waves, lat_plain, listed, base, back_pol)
    return (nonlinear, seed_next)


def local_small(seed_field, cotangent, step_size, owner_list):
    owner_count = lax.axis_size("ma")
    own_waves = cotangent.shape[3]
    norm_scale = 2.0 / math.sqrt(DEGREES * WAVES)
    block_width = min(128, WAVES)
    my_waves = lax.dynamic_slice_in_dim(owner_list, lax.axis_index("ma") * own_waves, own_waves)
    degree = jnp.arange(DEGREES, dtype=jnp.int32)
    live_cols = degree[:, None] >= my_waves[None, :]
    live_rows = jnp.transpose(live_cols)
    zero_value = jnp.zeros((), jnp.bfloat16)
    listed = jnp.take(seed_field, owner_list, axis=4)
    owned_seed = lax.all_to_all(listed, "ma", split_axis=4, concat_axis=3, tiled=True)
    lat_table = lat_cosines(jnp.arange(NLAT, dtype=jnp.int32))
    forward_rows = jnp.einsum(
        "crslk,tl->crstk",
        jnp.where(live_cols, owned_seed, zero_value),
        lat_table,
        preferred_element_type=jnp.float32,
    )
    adjoint_rows = jnp.einsum(
        "crskl,tl->crstk",
        jnp.where(live_rows, cotangent, zero_value),
        lat_table,
        preferred_element_type=jnp.float32,
    )
    spec_rows = jnp.concatenate([forward_rows, adjoint_rows], axis=0).astype(jnp.bfloat16)
    gridded = lax.all_to_all(
        lax.all_to_all(spec_rows, "ma", split_axis=3, concat_axis=4, tiled=True),
        "row",
        split_axis=3,
        concat_axis=1,
        tiled=True,
    )
    grid_field = None
    for start in range(0, WAVES, block_width):
        wave_block = wave_cosines(owner_list[start : start + block_width])
        partial_grid = jnp.einsum(
            "crsjm,smf->crjf",
            gridded[..., start : start + block_width],
            wave_block,
            preferred_element_type=jnp.float32,
        )
        grid_field = partial_grid if grid_field is None else grid_field + partial_grid
    grid_field = norm_scale * grid_field
    radial_pair = jnp.stack([grid_field[1], grid_field[3]])
    padded = jnp.pad(radial_pair, ((0, 0), (1, 1), (0, 0), (0, 0)))
    slopes = 0.5 * (padded[:, 2:] - padded[:, :-2])
    vel_tor = grid_field[0]
    mag_tor = grid_field[2]
    adj_vel = grid_field[4]
    adj_mag = grid_field[5]
    vel_pol = slopes[0]
    mag_pol = slopes[1]
    term_vel = mag_tor * mag_pol - vel_tor * vel_pol
    term_mag = vel_tor * mag_pol - vel_pol * mag_tor
    grad_vtor = -vel_pol * adj_vel + mag_pol * adj_mag
    grad_vpol = -vel_tor * adj_vel - mag_tor * adj_mag
    grad_mtor = mag_pol * adj_vel - vel_pol * adj_mag
    grad_mpol = mag_tor * adj_vel + vel_tor * adj_mag
    cotangent_pair = jnp.stack([grad_vpol, grad_mpol])
    padded_back = jnp.pad(cotangent_pair, ((0, 0), (1, 1), (0, 0), (0, 0)))
    back_slopes = 0.5 * (padded_back[:, :-2] - padded_back[:, 2:])
    analysis_in = jnp.stack(
        [term_vel, term_mag, grad_vtor, back_slopes[0], grad_mtor, back_slopes[1]]
    ).astype(jnp.bfloat16)
    spectra_parts = []
    for start in range(0, WAVES, block_width):
        wave_block = wave_cosines(owner_list[start : start + block_width])
        spectra_parts.append(
            jnp.einsum(
                "crjf,smf->crsjm", analysis_in, wave_block, preferred_element_type=jnp.float32
            )
        )
    spectra = (norm_scale * jnp.concatenate(spectra_parts, axis=4)).astype(jnp.bfloat16)
    position = jnp.arange(NLAT, dtype=jnp.int32)
    returned = lax.all_to_all(
        lax.all_to_all(spectra, "ma", split_axis=4, concat_axis=3, tiled=True),
        "row",
        split_axis=1,
        concat_axis=3,
        tiled=True,
    )
    sub_rows = spectra.shape[3]
    radial_part = position // (owner_count * sub_rows)
    owner_part = position // sub_rows % owner_count
    theta_index = owner_part * (NLAT // owner_count) + radial_part * sub_rows + position % sub_rows
    back_table = lat_cosines(theta_index)
    result = jnp.einsum("crstk,tl->crskl", returned, back_table, preferred_element_type=jnp.float32)
    result = jnp.where(live_rows, result, 0.0)
    nonlinear = result[:2]
    seed_next = jnp.swapaxes(owned_seed, 3, 4).astype(jnp.float32) - step_size[0] * result[2:]
    return (nonlinear, seed_next)


def fits(mesh):
    owners = mesh.shape["ma"]
    whole_tiles = all(size // owners % 128 == 0 for size in (WAVES, DEGREES, NLAT))
    return whole_tiles and owners >= 4 and owners & (owners - 1) == 0


def solution(mesh):
    return jax.shard_map(
        local if fits(mesh) else local_small,
        mesh=mesh,
        in_specs=(P(None, "row", None, "ma", None), P(None, "row", None, "ma", None), P(), P()),
        out_specs=(P(None, "row", None, "ma", None), P(None, "row", None, "ma", None)),
        check_vma=False,
    )
```

```python
import functools
import math

import jax
import jax.numpy as jnp
from jax import lax
from jax.experimental import pallas as pl
from jax.experimental.pallas import tpu as pltpu
from jax.sharding import PartitionSpec as P

WAVES = 1024
DEGREES = 1024
NLAT = 1024
NLON = 2048
F_TILE = 256
BF16 = jnp.bfloat16
F32 = jnp.float32


def lat_cosines(theta_index):
    degree = jnp.arange(DEGREES, dtype=jnp.int32)
    phase_index = (2 * theta_index[:, None] + 1) * degree[None, :] % (4 * NLAT)
    return jnp.cos(phase_index.astype(jnp.float32) * (math.pi / (2 * NLAT))).astype(jnp.bfloat16)


def wave_cosines(wave_ids):
    points = jnp.arange(NLON, dtype=jnp.int32)
    phase_index = wave_ids[:, None] * points[None, :] % NLON
    angles = phase_index.astype(jnp.float32) * (2.0 * math.pi / NLON)
    return jnp.stack([jnp.cos(angles), -jnp.sin(angles)]).astype(jnp.bfloat16)


def cos_sin(phase_index, period):
    angles = (phase_index % period).astype(F32) * (2.0 * math.pi / period)
    return jnp.cos(angles), jnp.sin(angles)


def lat_table_of(coarse, degree, step):
    fine = jnp.arange(step, dtype=jnp.int32)
    cos_a, sin_a = cos_sin(2 * step * coarse[:, None] * degree[None, :], 4 * NLAT)
    cos_b, sin_b = cos_sin((2 * fine[:, None] + 1) * degree[None, :], 4 * NLAT)
    table = cos_a[:, None, :] * cos_b[None, :, :] - sin_a[:, None, :] * sin_b[None, :, :]
    return table.astype(BF16).reshape(coarse.shape[0] * step, degree.shape[0])


def wave_tables_of(waves):
    tiles = jnp.arange(NLON // 2 // F_TILE, dtype=jnp.int32)
    fine = jnp.arange(F_TILE, dtype=jnp.int32)
    cos_a, sin_a = cos_sin(F_TILE * tiles[:, None] * waves[None, :], NLON)
    cos_b, sin_b = cos_sin(waves[:, None] * fine[None, :], NLON)
    cos_a, sin_a = cos_a[:, :, None], sin_a[:, :, None]
    cosine = cos_a * cos_b[None] - sin_a * sin_b[None]
    minus_sine = -sin_a * cos_b[None] - cos_a * sin_b[None]
    return cosine.astype(BF16), minus_sine.astype(BF16)


def middle_column_of(waves):
    sign = (1 - 2 * (waves % 2)).astype(BF16)
    column = jnp.arange(128, dtype=jnp.int32)
    return jnp.where(column[None, :] == 0, sign[:, None], jnp.zeros((), BF16))


def estimate(flops, bytes_accessed):
    return pl.CostEstimate(flops=int(flops), bytes_accessed=int(bytes_accessed), transcendentals=0)


def whole(shape):
    return pl.BlockSpec(shape, lambda *_: (0,) * len(shape))


def permute_kernel(owner_ref, seed_ref, *out_refs):
    chans, _, parts, lines, waves = seed_ref.shape
    own = out_refs[0].shape[-1]
    me = lax.axis_index("ma")
    rows = seed_ref[...].reshape(chans * parts * lines, waves)
    wave = lax.broadcasted_iota(jnp.int32, (waves, 2 * own), 0)
    for k in reversed(range(0, len(out_refs), 2)):
        wanted = jnp.concatenate(
            [owner_ref[pl.ds(me ^ k, 1), :], owner_ref[pl.ds(me ^ (k + 1), 1), :]], axis=1
        )
        one_hot = jnp.where(wave == wanted, 1.0, 0.0).astype(BF16)
        picked = jnp.dot(rows, one_hot, preferred_element_type=F32).astype(BF16)
        for d in range(2):
            part = picked[:, d * own : (d + 1) * own]
            out_refs[k + d][...] = part.reshape(chans, parts, lines, own)


def permute(seed_field, owner_list, owners):
    chans, _, parts, lines, waves = seed_field.shape
    own = waves // owners
    slot = jax.ShapeDtypeStruct((chans, parts, lines, own), BF16)
    return pl.pallas_call(
        permute_kernel,
        out_shape=[slot] * owners,
        cost_estimate=estimate(2 * seed_field.size * waves, 4 * seed_field.size),
        name="permute",
    )(owner_list.reshape(owners, own), seed_field)


def adjoint_rows_kernel(waves_ref, lat_ref, cot_ref, out_ref):
    parts, own, degrees = cot_ref.shape[2:]
    devices, _, _, sub, _ = out_ref.shape
    live = lax.broadcasted_iota(jnp.int32, (own, degrees), 1) >= waves_ref[...]
    for s in range(parts):
        coeffs = jnp.where(live, cot_ref[0, 0, s], jnp.zeros((), BF16))
        rows = lax.dot_general(
            lat_ref[...], coeffs, (((1,), (1,)), ((), ())), preferred_element_type=F32
        )
        out_ref[:, 0, s] = rows.astype(BF16).reshape(devices, sub, own)


def adjoint_rows(my_waves, lat_table, cotangent, seed_chans, devices):
    chans, _, parts, own, degrees = cotangent.shape
    sub = NLAT // devices
    return pl.pallas_call(
        adjoint_rows_kernel,
        grid=(chans,),
        in_specs=[
            pl.BlockSpec((own, 1), lambda c: (0, 0)),
            pl.BlockSpec((NLAT, degrees), lambda c: (0, 0)),
            pl.BlockSpec((1, 1, parts, own, degrees), lambda c: (c, 0, 0, 0, 0)),
        ],
        out_specs=pl.BlockSpec(
            (devices, 1, parts, sub, own), lambda c: (0, seed_chans + c, 0, 0, 0)
        ),
        out_shape=jax.ShapeDtypeStruct((devices, seed_chans + chans, parts, sub, own), BF16),
        cost_estimate=estimate(2 * cotangent.size * NLAT, 4 * cotangent.size + 2 * lat_table.size),
        name="adjoint_rows",
    )(my_waves.reshape(own, 1), lat_table, cotangent)


def forward_kernel(owners, waves_ref, lat_ref, base_ref, *refs):
    del base_ref
    seed_refs, out_ref = refs[:owners], refs[owners]
    _, parts, lines, own = seed_refs[0].shape
    devices, _, _, sub, _ = out_ref.shape
    me = lax.axis_index("ma")
    line = lax.broadcasted_iota(jnp.int32, (lines, own), 0)
    live = [line + (me ^ k) * lines >= waves_ref[...] for k in range(owners)]
    coeffs = jnp.concatenate(
        [
            jnp.concatenate(
                [
                    jnp.where(live[k], seed_refs[k][0, s], jnp.zeros((), BF16))
                    for k in range(owners)
                ],
                axis=0,
            )
            for s in range(parts)
        ],
        axis=1,
    )
    rows = jnp.dot(lat_ref[...], coeffs, preferred_element_type=F32).astype(BF16)
    for s in range(parts):
        out_ref[:, 0, s] = rows[:, s * own : (s + 1) * own].reshape(devices, sub, own)


def forward_rows(my_waves, lat_table, owned_seed, base):
    owners = len(owned_seed)
    chans, parts, lines, own = owned_seed[0].shape
    devices, _, _, sub, _ = base.shape
    size = owners * owned_seed[0].size
    return pl.pallas_call(
        functools.partial(forward_kernel, owners),
        grid=(chans,),
        in_specs=[
            whole((1, own)),
            whole(lat_table.shape),
            pl.BlockSpec(memory_space=pl.ANY),
        ]
        + [pl.BlockSpec((1, parts, lines, own), lambda c: (c, 0, 0, 0))] * owners,
        out_specs=pl.BlockSpec((devices, 1, parts, sub, own), lambda c: (0, c, 0, 0, 0)),
        out_shape=jax.ShapeDtypeStruct(base.shape, BF16),
        input_output_aliases={2: 0},
        cost_estimate=estimate(2 * size * NLAT, 4 * size + 2 * lat_table.size),
        name="forward_rows",
    )(my_waves.reshape(1, own), lat_table, base, *owned_seed)


def slope(values):
    rim = jnp.zeros_like(values[:1])
    upper = jnp.concatenate([values[1:], rim], axis=0)
    lower = jnp.concatenate([rim, values[:-1]], axis=0)
    return 0.5 * (upper - lower)


def products(field):
    vel_tor = field[0]
    vel_pol = slope(field[1])
    mag_tor = field[2]
    mag_pol = slope(field[3])
    adj_vel = field[4]
    adj_mag = field[5]
    grad_vpol = -vel_tor * adj_vel - mag_tor * adj_mag
    grad_mpol = mag_tor * adj_vel + vel_tor * adj_mag
    return [
        mag_tor * mag_pol - vel_tor * vel_pol,
        vel_tor * mag_pol - vel_pol * mag_tor,
        -vel_pol * adj_vel + mag_pol * adj_mag,
        -slope(grad_vpol),
        mag_pol * adj_vel - vel_pol * adj_mag,
        -slope(grad_mpol),
    ]


def grid_kernel(norm_scale, got_ref, cos_ref, sin_ref, mid_ref, back_cos_ref, back_sin_ref, back_mid_ref, out_ref, rows_ref, terms_ref, mid_terms_ref):
    step = pl.program_id(0)
    devices, chans, parts, sub, own = got_ref.shape
    radii = rows_ref.shape[2]
    f_tiles = terms_ref.shape[1]
    owners = devices // radii
    rows = chans * radii * sub
    group = out_ref.shape[0] // radii
    even, odd = 0, 1

    @pl.when(step == 0)
    def _():
        for s in range(parts):
            for d in range(owners):
                for r in range(radii):
                    rows_ref[s, :, r, :, d * own : (d + 1) * own] = got_ref[d * radii + r, :, s]

    def rows_of(s):
        return rows_ref[s].reshape(rows, owners * own)

    @pl.when(step < f_tiles)
    def _():
        cosines = norm_scale * jnp.dot(rows_of(even), cos_ref[0], preferred_element_type=F32)
        sines = norm_scale * jnp.dot(rows_of(odd), sin_ref[0], preferred_element_type=F32)
        shape = (chans, radii, sub, F_TILE)
        plus = products((cosines + sines).reshape(shape))
        minus = products((cosines - sines).reshape(shape))
        column = lax.broadcasted_iota(jnp.int32, (radii, sub, F_TILE), 2)
        paired = (column > 0) | (step > 0)
        for c in range(chans):
            mirror = jnp.where(paired, minus[c], 0.0)
            terms_ref[even, step, c] = (plus[c] + mirror).astype(BF16)
            terms_ref[odd, step, c] = (plus[c] - mirror).astype(BF16)

    @pl.when(step == f_tiles)
    def _():
        field = norm_scale * jnp.dot(rows_of(even), mid_ref[...], preferred_element_type=F32)
        for c, term in enumerate(products(field.reshape(chans, radii, sub, -1))):
            mid_terms_ref[c] = term.astype(BF16)

    def analyse(s, table_ref):
        total = None
        for a in range(f_tiles):
            part = lax.dot_general(
                terms_ref[s, a].reshape(rows, F_TILE),
                table_ref[a],
                (((1,), (1,)), ((), ())),
                preferred_element_type=F32,
            )
            total = part if total is None else total + part
        return total

    def put(s, total):
        back = (norm_scale * total).astype(BF16).reshape(chans, radii, sub, group * own)
        for d in range(group):
            for r in range(radii):
                out_ref[d * radii + r, :, s] = back[:, r, :, d * own : (d + 1) * own]

    @pl.when(step > f_tiles)
    def _():
        middle = lax.dot_general(
            mid_terms_ref[...].reshape(rows, -1),
            back_mid_ref[...],
            (((1,), (1,)), ((), ())),
            preferred_element_type=F32,
        )
        put(even, analyse(even, back_cos_ref) + middle)
        put(odd, analyse(odd, back_sin_ref))


def grid_step(got, cosine, minus_sine, middle, radii):
    devices, chans, parts, sub, own = got.shape
    owners = devices // radii
    f_tiles, waves, _ = cosine.shape
    group = 2
    norm_scale = 2.0 / math.sqrt(DEGREES * WAVES)

    def back(i):
        return jnp.maximum(i - f_tiles - 1, 0)

    ahead = pl.BlockSpec((1, waves, F_TILE), lambda i: (jnp.minimum(i, f_tiles - 1), 0, 0))
    behind = pl.BlockSpec((f_tiles, group * own, F_TILE), lambda i: (0, back(i), 0))
    return pl.pallas_call(
        functools.partial(grid_kernel, norm_scale),
        grid=(f_tiles + 1 + owners // group,),
        in_specs=[
            whole(got.shape),
            ahead,
            ahead,
            whole(middle.shape),
            behind,
            behind,
            pl.BlockSpec((group * own, middle.shape[1]), lambda i: (back(i), 0)),
        ],
        out_specs=pl.BlockSpec(
            (group * radii, chans, parts, sub, own), lambda i: (back(i), 0, 0, 0, 0)
        ),
        out_shape=jax.ShapeDtypeStruct(got.shape, BF16),
        scratch_shapes=[
            pltpu.VMEM((parts, chans, radii, sub, waves), BF16),
            pltpu.VMEM((parts, f_tiles, chans, radii, sub, F_TILE), BF16),
            pltpu.VMEM((chans, radii, sub, middle.shape[1]), BF16),
        ],
        cost_estimate=estimate(
            4 * chans * radii * sub * waves * NLON, 4 * got.size + 8 * cosine.size
        ),
        name="grid_step",
    )(got, cosine, minus_sine, middle, cosine, minus_sine, middle)


def listed_kernel(*refs):
    owners = len(refs) - 1
    out_ref = refs[owners]
    _, parts, lines, own = refs[0].shape
    me = lax.axis_index("ma")
    for k in range(owners):
        column = pl.multiple_of((me ^ k) * lines, lines)
        for s in range(parts):
            out_ref[0, s, :, pl.ds(column, lines)] = refs[k][0, s].astype(F32).T.astype(BF16)


def list_seed(owned_seed):
    owners = len(owned_seed)
    chans, parts, lines, own = owned_seed[0].shape
    return pl.pallas_call(
        listed_kernel,
        grid=(chans,),
        in_specs=[pl.BlockSpec((1, parts, lines, own), lambda c: (c, 0, 0, 0))] * owners,
        out_specs=pl.BlockSpec((1, parts, own, owners * lines), lambda c: (c, 0, 0, 0)),
        out_shape=jax.ShapeDtypeStruct((chans, parts, own, owners * lines), BF16),
        cost_estimate=estimate(0, 4 * owners * owned_seed[0].size),
        name="list_seed",
    )(*owned_seed)


def result_kernel(pair, step_ref, waves_ref, lat_ref, back_ref, listed_ref, non_ref, next_ref):
    block = pl.program_id(0)
    devices, _, parts, sub, own = back_ref.shape
    degrees = lat_ref.shape[1]
    live = lax.broadcasted_iota(jnp.int32, (own, degrees), 1) >= waves_ref[...]
    columns = jnp.concatenate(
        [
            back_ref[:, c, s].reshape(devices * sub, own)
            for c in range(pair)
            for s in range(parts)
        ],
        axis=1,
    )
    result = lax.dot_general(
        columns, lat_ref[...], (((0,), (0,)), ((), ())), preferred_element_type=F32
    )
    for c in range(pair):
        for s in range(parts):
            start = (c * parts + s) * own
            value = jnp.where(live, result[start : start + own], 0.0)

            @pl.when(block == 0)
            def _(value=value, c=c, s=s):
                non_ref[c, 0, s] = value

            @pl.when(block > 0)
            def _(value=value, c=c, s=s):
                next_ref[c, 0, s] = listed_ref[c, s].astype(F32) - step_ref[0] * value


def results(step_size, my_waves, lat_table, returned, listed):
    devices, chans, parts, sub, own = returned.shape
    degrees = lat_table.shape[1]
    pair = 2
    seed_chans = listed.shape[0]

    def seed_block(i):
        return jnp.maximum(i - 1, 0)

    return pl.pallas_call(
        functools.partial(result_kernel, pair),
        grid=(chans // pair,),
        in_specs=[
            pl.BlockSpec(memory_space=pltpu.SMEM),
            pl.BlockSpec((own, 1), lambda i: (0, 0)),
            pl.BlockSpec(lat_table.shape, lambda i: (0, 0)),
            pl.BlockSpec((devices, pair, parts, sub, own), lambda i: (0, i, 0, 0, 0)),
            pl.BlockSpec((pair, parts, own, degrees), lambda i: (seed_block(i), 0, 0, 0)),
        ],
        out_specs=[
            pl.BlockSpec((pair, 1, parts, own, degrees), lambda i: (0, 0, 0, 0, 0)),
            pl.BlockSpec((pair, 1, parts, own, degrees), lambda i: (seed_block(i), 0, 0, 0, 0)),
        ],
        out_shape=[
            jax.ShapeDtypeStruct((chans - seed_chans, 1, parts, own, degrees), F32),
            jax.ShapeDtypeStruct((seed_chans, 1, parts, own, degrees), F32),
        ],
        cost_estimate=estimate(2 * returned.size * degrees, 2 * returned.size + 4 * returned.size),
        name="results",
    )(step_size, my_waves.reshape(own, 1), lat_table, returned, listed)


def exchange(slots):
    owners = len(slots)
    got = list(slots)
    for k in reversed(range(1, owners)):
        got[k] = lax.ppermute(slots[k], "ma", [(i, i ^ k) for i in range(owners)])
    return got


def local(seed_field, cotangent, step_size, owner_list):
    owners, radii = lax.axis_size("ma"), lax.axis_size("row")
    own = cotangent.shape[3]
    me = lax.axis_index("ma")
    my_waves = lax.dynamic_slice_in_dim(owner_list, me * own, own)
    owned_seed = exchange(permute(seed_field, owner_list, owners))
    lines, step = DEGREES // owners, 32
    slot_ids = me ^ jnp.arange(owners, dtype=jnp.int32)
    lines_of = jnp.arange(lines, dtype=jnp.int32)
    slot_degree = (slot_ids[:, None] * lines + lines_of[None, :]).reshape(-1)
    coarse = jnp.arange(NLAT // step, dtype=jnp.int32)
    lat_plain = lat_table_of(coarse, jnp.arange(DEGREES, dtype=jnp.int32), step)
    lat_slots = lat_table_of(coarse, slot_degree, step)
    cosine, minus_sine = wave_tables_of(owner_list)
    middle = middle_column_of(owner_list)
    base = adjoint_rows(my_waves, lat_plain, cotangent, seed_field.shape[0], owners * radii)
    spec_rows = forward_rows(my_waves, lat_slots, owned_seed, base)
    gridded = lax.all_to_all(spec_rows, ("ma", "row"), 0, 0, tiled=True)
    listed = list_seed(owned_seed)
    back_rows = grid_step(gridded, cosine, minus_sine, middle, radii)
    returned = lax.all_to_all(back_rows, ("ma", "row"), 0, 0, tiled=True)
    nonlinear, seed_next = results(step_size, my_waves, lat_plain, returned, listed)
    return (nonlinear, seed_next)


def local_small(seed_field, cotangent, step_size, owner_list):
    owner_count = lax.axis_size("ma")
    own_waves = cotangent.shape[3]
    norm_scale = 2.0 / math.sqrt(DEGREES * WAVES)
    block_width = min(128, WAVES)
    my_waves = lax.dynamic_slice_in_dim(owner_list, lax.axis_index("ma") * own_waves, own_waves)
    degree = jnp.arange(DEGREES, dtype=jnp.int32)
    live_cols = degree[:, None] >= my_waves[None, :]
    live_rows = jnp.transpose(live_cols)
    zero_value = jnp.zeros((), jnp.bfloat16)
    listed = jnp.take(seed_field, owner_list, axis=4)
    owned_seed = lax.all_to_all(listed, "ma", split_axis=4, concat_axis=3, tiled=True)
    lat_table = lat_cosines(jnp.arange(NLAT, dtype=jnp.int32))
    forward_rows = jnp.einsum(
        "crslk,tl->crstk",
        jnp.where(live_cols, owned_seed, zero_value),
        lat_table,
        preferred_element_type=jnp.float32,
    )
    adjoint_rows = jnp.einsum(
        "crskl,tl->crstk",
        jnp.where(live_rows, cotangent, zero_value),
        lat_table,
        preferred_element_type=jnp.float32,
    )
    spec_rows = jnp.concatenate([forward_rows, adjoint_rows], axis=0).astype(jnp.bfloat16)
    gridded = lax.all_to_all(
        lax.all_to_all(spec_rows, "ma", split_axis=3, concat_axis=4, tiled=True),
        "row",
        split_axis=3,
        concat_axis=1,
        tiled=True,
    )
    grid_field = None
    for start in range(0, WAVES, block_width):
        wave_block = wave_cosines(owner_list[start : start + block_width])
        partial_grid = jnp.einsum(
            "crsjm,smf->crjf",
            gridded[..., start : start + block_width],
            wave_block,
            preferred_element_type=jnp.float32,
        )
        grid_field = partial_grid if grid_field is None else grid_field + partial_grid
    grid_field = norm_scale * grid_field
    radial_pair = jnp.stack([grid_field[1], grid_field[3]])
    padded = jnp.pad(radial_pair, ((0, 0), (1, 1), (0, 0), (0, 0)))
    slopes = 0.5 * (padded[:, 2:] - padded[:, :-2])
    vel_tor = grid_field[0]
    mag_tor = grid_field[2]
    adj_vel = grid_field[4]
    adj_mag = grid_field[5]
    vel_pol = slopes[0]
    mag_pol = slopes[1]
    term_vel = mag_tor * mag_pol - vel_tor * vel_pol
    term_mag = vel_tor * mag_pol - vel_pol * mag_tor
    grad_vtor = -vel_pol * adj_vel + mag_pol * adj_mag
    grad_vpol = -vel_tor * adj_vel - mag_tor * adj_mag
    grad_mtor = mag_pol * adj_vel - vel_pol * adj_mag
    grad_mpol = mag_tor * adj_vel + vel_tor * adj_mag
    cotangent_pair = jnp.stack([grad_vpol, grad_mpol])
    padded_back = jnp.pad(cotangent_pair, ((0, 0), (1, 1), (0, 0), (0, 0)))
    back_slopes = 0.5 * (padded_back[:, :-2] - padded_back[:, 2:])
    analysis_in = jnp.stack(
        [term_vel, term_mag, grad_vtor, back_slopes[0], grad_mtor, back_slopes[1]]
    ).astype(jnp.bfloat16)
    spectra_parts = []
    for start in range(0, WAVES, block_width):
        wave_block = wave_cosines(owner_list[start : start + block_width])
        spectra_parts.append(
            jnp.einsum(
                "crjf,smf->crsjm", analysis_in, wave_block, preferred_element_type=jnp.float32
            )
        )
    spectra = (norm_scale * jnp.concatenate(spectra_parts, axis=4)).astype(jnp.bfloat16)
    position = jnp.arange(NLAT, dtype=jnp.int32)
    returned = lax.all_to_all(
        lax.all_to_all(spectra, "ma", split_axis=4, concat_axis=3, tiled=True),
        "row",
        split_axis=1,
        concat_axis=3,
        tiled=True,
    )
    sub_rows = spectra.shape[3]
    radial_part = position // (owner_count * sub_rows)
    owner_part = position // sub_rows % owner_count
    theta_index = owner_part * (NLAT // owner_count) + radial_part * sub_rows + position % sub_rows
    back_table = lat_cosines(theta_index)
    result = jnp.einsum("crstk,tl->crskl", returned, back_table, preferred_element_type=jnp.float32)
    result = jnp.where(live_rows, result, 0.0)
    nonlinear = result[:2]
    seed_next = jnp.swapaxes(owned_seed, 3, 4).astype(jnp.float32) - step_size[0] * result[2:]
    return (nonlinear, seed_next)


def fits(mesh):
    owners, radii = mesh.shape["ma"], mesh.shape["row"]
    own, sub = WAVES // owners, NLAT // (owners * radii)
    return own % 128 == 0 and sub % 16 == 0 and owners > 1 and owners & (owners - 1) == 0


def solution(mesh):
    return jax.shard_map(
        local if fits(mesh) else local_small,
        mesh=mesh,
        in_specs=(P(None, "row", None, "ma", None), P(None, "row", None, "ma", None), P(), P()),
        out_specs=(P(None, "row", None, "ma", None), P(None, "row", None, "ma", None)),
        check_vma=False,
    )
```

```python
import functools
import math

import jax
import jax.numpy as jnp
from jax import lax
from jax.experimental import pallas as pl
from jax.experimental.pallas import tpu as pltpu
from jax.sharding import PartitionSpec as P

WAVES = 1024
DEGREES = 1024
NLAT = 1024
NLON = 2048
F_TILE = 512
LANES = 128
BF16 = jnp.bfloat16
F32 = jnp.float32


def lat_cosines(theta_index):
    degree = jnp.arange(DEGREES, dtype=jnp.int32)
    phase_index = (2 * theta_index[:, None] + 1) * degree[None, :] % (4 * NLAT)
    return jnp.cos(phase_index.astype(jnp.float32) * (math.pi / (2 * NLAT))).astype(jnp.bfloat16)


def wave_cosines(wave_ids):
    points = jnp.arange(NLON, dtype=jnp.int32)
    phase_index = wave_ids[:, None] * points[None, :] % NLON
    angles = phase_index.astype(jnp.float32) * (2.0 * math.pi / NLON)
    return jnp.stack([jnp.cos(angles), -jnp.sin(angles)]).astype(jnp.bfloat16)


def cos_sin(phase_index, period):
    angles = (phase_index % period).astype(F32) * (2.0 * math.pi / period)
    return jnp.cos(angles), jnp.sin(angles)


def lat_table_of(coarse, degree, step):
    fine = jnp.arange(step, dtype=jnp.int32)
    cos_a, sin_a = cos_sin(2 * step * coarse[:, None] * degree[None, :], 4 * NLAT)
    cos_b, sin_b = cos_sin((2 * fine[:, None] + 1) * degree[None, :], 4 * NLAT)
    table = cos_a[:, None, :] * cos_b[None, :, :] - sin_a[:, None, :] * sin_b[None, :, :]
    return table.astype(BF16).reshape(coarse.shape[0] * step, degree.shape[0])


def wave_tables_of(waves, scale):
    tiles = jnp.arange(NLON // 2 // F_TILE, dtype=jnp.int32)
    fine = jnp.arange(F_TILE, dtype=jnp.int32)
    cos_a, sin_a = cos_sin(F_TILE * tiles[:, None] * waves[None, :], NLON)
    cos_b, sin_b = cos_sin(waves[:, None] * fine[None, :], NLON)
    cos_a, sin_a = cos_a[:, :, None], sin_a[:, :, None]
    cosine = cos_a * cos_b[None] - sin_a * sin_b[None]
    minus_sine = -sin_a * cos_b[None] - cos_a * sin_b[None]
    return scale * cosine.astype(BF16), scale * minus_sine.astype(BF16)


def middle_column_of(waves, scale):
    sign = scale * (1 - 2 * (waves % 2)).astype(BF16)
    column = jnp.arange(LANES, dtype=jnp.int32)
    return jnp.where(column[None, :] == 0, sign[:, None], jnp.zeros((), BF16))


def estimate(flops, bytes_accessed):
    return pl.CostEstimate(flops=int(flops), bytes_accessed=int(bytes_accessed), transcendentals=0)


def whole(shape):
    return pl.BlockSpec(shape, lambda *_: (0,) * len(shape))


def permute_kernel(first, owner_ref, seed_ref, *out_refs):
    chans, _, parts, lines, waves = seed_ref.shape
    own = out_refs[0].shape[-1]
    me = lax.axis_index("ma")
    rows = seed_ref[...].reshape(chans * parts * lines, waves)
    wave = lax.broadcasted_iota(jnp.int32, (waves, len(out_refs) * own), 0)
    wanted = jnp.concatenate(
        [owner_ref[pl.ds(me ^ (first + k), 1), :] for k in range(len(out_refs))], axis=1
    )
    one_hot = jnp.where(wave == wanted, 1.0, 0.0).astype(BF16)
    picked = jnp.dot(rows, one_hot, preferred_element_type=F32).astype(BF16)
    for k, out_ref in enumerate(out_refs):
        out_ref[...] = picked[:, k * own : (k + 1) * own].reshape(chans, parts, lines, own)


def permute(seed_field, owner_list, owners, first, count):
    chans, _, parts, lines, waves = seed_field.shape
    own = waves // owners
    slot = jax.ShapeDtypeStruct((chans, parts, lines, own), BF16)
    return pl.pallas_call(
        functools.partial(permute_kernel, first),
        out_shape=[slot] * count,
        cost_estimate=estimate(2 * seed_field.size * own * count, 3 * seed_field.size),
        name="permute",
    )(owner_list.reshape(owners, own), seed_field)


def adjoint_rows_kernel(waves_ref, lat_ref, cot_ref, out_ref):
    parts, own, degrees = cot_ref.shape[2:]
    devices, _, _, sub, _ = out_ref.shape
    live = lax.broadcasted_iota(jnp.int32, (own, degrees), 1) >= waves_ref[...]
    for s in range(parts):
        coeffs = jnp.where(live, cot_ref[0, 0, s], jnp.zeros((), BF16))
        rows = lax.dot_general(
            lat_ref[...], coeffs, (((1,), (1,)), ((), ())), preferred_element_type=F32
        )
        out_ref[:, 0, s] = rows.astype(BF16).reshape(devices, sub, own)


def adjoint_rows(my_waves, lat_table, cotangent, devices):
    chans, _, parts, own, degrees = cotangent.shape
    sub = NLAT // devices
    return pl.pallas_call(
        adjoint_rows_kernel,
        grid=(chans,),
        in_specs=[
            pl.BlockSpec((own, 1), lambda c: (0, 0)),
            pl.BlockSpec((NLAT, degrees), lambda c: (0, 0)),
            pl.BlockSpec((1, 1, parts, own, degrees), lambda c: (c, 0, 0, 0, 0)),
        ],
        out_specs=pl.BlockSpec((devices, 1, parts, sub, own), lambda c: (0, c, 0, 0, 0)),
        out_shape=jax.ShapeDtypeStruct((devices, chans, parts, sub, own), BF16),
        cost_estimate=estimate(2 * cotangent.size * NLAT, 4 * cotangent.size + 2 * lat_table.size),
        name="adjoint_rows",
    )(my_waves.reshape(own, 1), lat_table, cotangent)


def forward_kernel(owners, waves_ref, lat_ref, *refs):
    seed_refs, out_ref = refs[:owners], refs[owners]
    chans, parts, lines, own = seed_refs[0].shape
    devices, _, _, sub, _ = out_ref.shape
    me = lax.axis_index("ma")
    line = lax.broadcasted_iota(jnp.int32, (lines, own), 0)
    live = [line + (me ^ k) * lines >= waves_ref[...] for k in range(owners)]
    columns = [(c, s) for c in range(chans) for s in range(parts)]
    coeffs = jnp.concatenate(
        [
            jnp.concatenate(
                [
                    jnp.where(live[k], seed_refs[k][c, s], jnp.zeros((), BF16))
                    for k in range(owners)
                ],
                axis=0,
            )
            for c, s in columns
        ],
        axis=1,
    )
    rows = jnp.dot(lat_ref[...], coeffs, preferred_element_type=F32).astype(BF16)
    for i, (c, s) in enumerate(columns):
        out_ref[:, c, s] = rows[:, i * own : (i + 1) * own].reshape(devices, sub, own)


def forward_rows(my_waves, lat_table, owned_seed, devices):
    owners = len(owned_seed)
    chans, parts, lines, own = owned_seed[0].shape
    sub = NLAT // devices
    size = owners * owned_seed[0].size
    return pl.pallas_call(
        functools.partial(forward_kernel, owners),
        grid=(chans // 2,),
        in_specs=[whole((1, own)), whole(lat_table.shape)]
        + [pl.BlockSpec((2, parts, lines, own), lambda c: (c, 0, 0, 0))] * owners,
        out_specs=pl.BlockSpec((devices, 2, parts, sub, own), lambda c: (0, c, 0, 0, 0)),
        out_shape=jax.ShapeDtypeStruct((devices, chans, parts, sub, own), BF16),
        cost_estimate=estimate(2 * size * NLAT, 4 * size + 2 * lat_table.size),
        name="forward_rows",
    )(my_waves.reshape(1, own), lat_table, *owned_seed)


def slope(values):
    rim = jnp.zeros_like(values[0])
    padded = [rim] + list(values) + [rim]
    return [0.5 * (padded[r + 2] - padded[r]) for r in range(len(values))]


def products(fields):
    vel_tor, mag_tor, adj_vel, adj_mag = fields[0], fields[2], fields[4], fields[5]
    vel_pol, mag_pol = slope(fields[1]), slope(fields[3])
    radii = range(len(vel_tor))
    grad_vpol = [-vel_tor[r] * adj_vel[r] - mag_tor[r] * adj_mag[r] for r in radii]
    grad_mpol = [mag_tor[r] * adj_vel[r] + vel_tor[r] * adj_mag[r] for r in radii]
    return [
        [mag_tor[r] * mag_pol[r] - vel_tor[r] * vel_pol[r] for r in radii],
        [vel_tor[r] * mag_pol[r] - vel_pol[r] * mag_tor[r] for r in radii],
        [-vel_pol[r] * adj_vel[r] + mag_pol[r] * adj_mag[r] for r in radii],
        [-value for value in slope(grad_vpol)],
        [mag_pol[r] * adj_vel[r] - vel_pol[r] * adj_mag[r] for r in radii],
        [-value for value in slope(grad_mpol)],
    ]


def grid_kernel(
    seed_ref,
    adj_ref,
    cos_ref,
    sin_ref,
    mid_ref,
    back_cos_ref,
    back_sin_ref,
    back_mid_ref,
    out_ref,
    rows_ref,
    cosines_ref,
    sines_ref,
    terms_ref,
    mid_terms_ref,
    sem_ref,
):
    step = pl.program_id(0)
    parts, radii, chans, sub, waves = rows_ref.shape
    f_tiles = terms_ref.shape[1]
    rows = radii * chans * sub
    group = out_ref.shape[0] // radii
    own = out_ref.shape[-1]
    owners = waves // own
    seed_chans = seed_ref.shape[1]
    even, odd = 0, 1
    piece = 16

    def copies():
        for g, (got_ref, first) in enumerate(((adj_ref, seed_chans), (seed_ref, 0))):
            for s in range(parts):
                for d in range(owners):
                    yield pltpu.make_async_copy(
                        got_ref.at[d * radii : (d + 1) * radii, :, s],
                        rows_ref.at[
                            s,
                            :,
                            first : first + got_ref.shape[1],
                            :,
                            d * own : (d + 1) * own,
                        ],
                        sem_ref.at[g, s, d],
                    )

    @pl.when(step == 0)
    def _():
        for copy in copies():
            copy.start()
        for copy in copies():
            copy.wait()

    def rows_of(s):
        return rows_ref[s].reshape(rows, waves)

    @pl.when(step < f_tiles)
    def _():
        shape = (radii, chans, sub, F_TILE)
        cosines_ref[...] = jnp.dot(
            rows_of(even), cos_ref[0], preferred_element_type=F32
        ).reshape(shape)
        sines_ref[...] = jnp.dot(rows_of(odd), sin_ref[0], preferred_element_type=F32).reshape(
            shape
        )

        @pl.loop(0, F_TILE // LANES)
        def _(tile):
            lanes = pl.ds(pl.multiple_of(tile * LANES, LANES), LANES)
            column = lax.broadcasted_iota(jnp.int32, (piece, LANES), 1)
            paired = column + (step * F_TILE + tile * LANES) > 0
            for start in range(0, sub, piece):
                lats = slice(start, start + piece)
                cosines = [
                    [cosines_ref[r, c, lats, lanes] for r in range(radii)] for c in range(chans)
                ]
                sines = [
                    [sines_ref[r, c, lats, lanes] for r in range(radii)] for c in range(chans)
                ]
                plus = products(
                    [[a + b for a, b in zip(*pair)] for pair in zip(cosines, sines)]
                )
                minus = products(
                    [[a - b for a, b in zip(*pair)] for pair in zip(cosines, sines)]
                )
                for c in range(chans):
                    for r in range(radii):
                        mirror = jnp.where(paired, minus[c][r], 0.0)
                        terms_ref[even, step, r, c, lats, lanes] = (plus[c][r] + mirror).astype(
                            BF16
                        )
                        terms_ref[odd, step, r, c, lats, lanes] = (plus[c][r] - mirror).astype(
                            BF16
                        )

    @pl.when(step == f_tiles)
    def _():
        cosines_ref[:, :, :, :LANES] = jnp.dot(
            rows_of(even), mid_ref[...], preferred_element_type=F32
        ).reshape(radii, chans, sub, LANES)
        for start in range(0, sub, piece):
            lats = slice(start, start + piece)
            field = [
                [cosines_ref[r, c, lats, :LANES] for r in range(radii)] for c in range(chans)
            ]
            for c, term in enumerate(products(field)):
                for r in range(radii):
                    mid_terms_ref[r, c, lats, :] = term[r].astype(BF16)

    def analyse(s, table_ref):
        total = None
        for a in range(f_tiles):
            part = lax.dot_general(
                terms_ref[s, a].reshape(rows, F_TILE),
                table_ref[a],
                (((1,), (1,)), ((), ())),
                preferred_element_type=F32,
            )
            total = part if total is None else total + part
        return total

    def put(s, total):
        back = total.astype(BF16).reshape(radii, chans, sub, group * own)
        for d in range(group):
            for r in range(radii):
                out_ref[d * radii + r, :, s] = back[r, :, :, d * own : (d + 1) * own]

    @pl.when(step > f_tiles)
    def _():
        middle = lax.dot_general(
            mid_terms_ref[...].reshape(rows, LANES),
            back_mid_ref[...],
            (((1,), (1,)), ((), ())),
            preferred_element_type=F32,
        )
        put(even, analyse(even, back_cos_ref) + middle)
        put(odd, analyse(odd, back_sin_ref))


def grid_step(seed_got, adj_got, cosine, minus_sine, middle, radii):
    devices, seed_chans, parts, sub, own = seed_got.shape
    chans = seed_chans + adj_got.shape[1]
    owners = devices // radii
    f_tiles, waves, _ = cosine.shape
    group = 2

    def back(i):
        return jnp.maximum(i - f_tiles - 1, 0)

    ahead = pl.BlockSpec((1, waves, F_TILE), lambda i: (jnp.minimum(i, f_tiles - 1), 0, 0))
    behind = pl.BlockSpec((f_tiles, group * own, F_TILE), lambda i: (0, back(i), 0))
    return pl.pallas_call(
        grid_kernel,
        grid=(f_tiles + 1 + owners // group,),
        in_specs=[
            pl.BlockSpec(memory_space=pl.ANY),
            pl.BlockSpec(memory_space=pl.ANY),
            ahead,
            ahead,
            whole(middle.shape),
            behind,
            behind,
            pl.BlockSpec((group * own, LANES), lambda i: (back(i), 0)),
        ],
        out_specs=pl.BlockSpec(
            (group * radii, chans, parts, sub, own), lambda i: (back(i), 0, 0, 0, 0)
        ),
        out_shape=jax.ShapeDtypeStruct((devices, chans, parts, sub, own), BF16),
        scratch_shapes=[
            pltpu.VMEM((parts, radii, chans, sub, waves), BF16),
            pltpu.VMEM((radii, chans, sub, F_TILE), F32),
            pltpu.VMEM((radii, chans, sub, F_TILE), F32),
            pltpu.VMEM((parts, f_tiles, radii, chans, sub, F_TILE), BF16),
            pltpu.VMEM((radii, chans, sub, LANES), BF16),
            pltpu.SemaphoreType.DMA((2, parts, owners)),
        ],
        cost_estimate=estimate(
            4 * chans * radii * sub * waves * NLON, 6 * seed_got.size + 8 * cosine.size
        ),
        name="grid_step",
    )(seed_got, adj_got, cosine, minus_sine, middle, cosine, minus_sine, middle)


def listed_kernel(*refs):
    owners = len(refs) - 1
    out_ref = refs[owners]
    _, parts, lines, own = refs[0].shape
    me = lax.axis_index("ma")
    for k in range(owners):
        column = pl.multiple_of((me ^ k) * lines, lines)
        for s in range(parts):
            out_ref[0, s, :, pl.ds(column, lines)] = refs[k][0, s].astype(F32).T.astype(BF16)


def list_seed(owned_seed):
    owners = len(owned_seed)
    chans, parts, lines, own = owned_seed[0].shape
    return pl.pallas_call(
        listed_kernel,
        grid=(chans,),
        in_specs=[pl.BlockSpec((1, parts, lines, own), lambda c: (c, 0, 0, 0))] * owners,
        out_specs=pl.BlockSpec((1, parts, own, owners * lines), lambda c: (c, 0, 0, 0)),
        out_shape=jax.ShapeDtypeStruct((chans, parts, own, owners * lines), BF16),
        cost_estimate=estimate(0, 4 * owners * owned_seed[0].size),
        name="list_seed",
    )(*owned_seed)


def result_kernel(seed_chans, step_ref, waves_ref, lat_ref, back_ref, listed_ref, non_ref, next_ref, cols_ref, lhs_ref, sem_ref):
    tile = pl.program_id(0)
    devices, chans, parts, sub, own = back_ref.shape
    width = lat_ref.shape[1]
    columns = [(c, s) for c in range(chans) for s in range(parts)]

    @pl.when(tile == 0)
    def _():
        copies = [
            pltpu.make_async_copy(back_ref.at[:, c, s], cols_ref.at[i], sem_ref.at[i])
            for i, (c, s) in enumerate(columns)
        ]
        for copy in copies:
            copy.start()
        for i, copy in enumerate(copies):
            copy.wait()
            lhs_ref[i] = cols_ref[i].reshape(devices * sub, own).T

    degree = lax.broadcasted_iota(jnp.int32, (own, width), 1) + tile * width
    live = degree >= waves_ref[...]
    for i, (c, s) in enumerate(columns):
        result = jnp.dot(lhs_ref[i], lat_ref[...], preferred_element_type=F32)
        value = jnp.where(live, result, 0.0)
        seed_chan = c - (chans - seed_chans)
        if seed_chan < 0:
            non_ref[c, 0, s] = value
        else:
            next_ref[seed_chan, 0, s] = listed_ref[seed_chan, s].astype(F32) - step_ref[0] * value


def results(step_size, my_waves, lat_table, returned, listed):
    devices, chans, parts, sub, own = returned.shape
    degrees = lat_table.shape[1]
    width = 256
    seed_chans = listed.shape[0]
    return pl.pallas_call(
        functools.partial(result_kernel, seed_chans),
        grid=(degrees // width,),
        in_specs=[
            pl.BlockSpec(memory_space=pltpu.SMEM),
            whole((own, 1)),
            pl.BlockSpec((NLAT, width), lambda i: (0, i)),
            pl.BlockSpec(memory_space=pl.ANY),
            pl.BlockSpec((seed_chans, parts, own, width), lambda i: (0, 0, 0, i)),
        ],
        out_specs=[
            pl.BlockSpec((chans - seed_chans, 1, parts, own, width), lambda i: (0, 0, 0, 0, i)),
            pl.BlockSpec((seed_chans, 1, parts, own, width), lambda i: (0, 0, 0, 0, i)),
        ],
        out_shape=[
            jax.ShapeDtypeStruct((chans - seed_chans, 1, parts, own, degrees), F32),
            jax.ShapeDtypeStruct((seed_chans, 1, parts, own, degrees), F32),
        ],
        scratch_shapes=[
            pltpu.VMEM((chans * parts, devices, sub, own), BF16),
            pltpu.VMEM((chans * parts, own, devices * sub), BF16),
            pltpu.SemaphoreType.DMA((chans * parts,)),
        ],
        cost_estimate=estimate(2 * returned.size * degrees, 6 * returned.size),
        name="results",
    )(step_size, my_waves.reshape(own, 1), lat_table, returned, listed)


def exchange(slots):
    owners = len(slots)
    got = list(slots)
    for k in reversed(range(1, owners)):
        got[k] = lax.ppermute(slots[k], "ma", [(i, i ^ k) for i in range(owners)])
    return got


def local(seed_field, cotangent, step_size, owner_list):
    owners, radii = lax.axis_size("ma"), lax.axis_size("row")
    own = cotangent.shape[3]
    norm_scale = 2.0 / math.sqrt(DEGREES * WAVES)
    me = lax.axis_index("ma")
    my_waves = lax.dynamic_slice_in_dim(owner_list, me * own, own)
    half = owners // 2
    far = permute(seed_field, owner_list, owners, half, half)
    near = permute(seed_field, owner_list, owners, 0, half)
    owned_seed = exchange(list(near) + list(far))
    lines, step = DEGREES // owners, 32
    slot_ids = me ^ jnp.arange(owners, dtype=jnp.int32)
    lines_of = jnp.arange(lines, dtype=jnp.int32)
    slot_degree = (slot_ids[:, None] * lines + lines_of[None, :]).reshape(-1)
    coarse = jnp.arange(NLAT // step, dtype=jnp.int32)
    lat_plain = lat_table_of(coarse, jnp.arange(DEGREES, dtype=jnp.int32), step)
    lat_slots = lat_table_of(coarse, slot_degree, step)
    cosine, minus_sine = wave_tables_of(owner_list, norm_scale)
    middle = middle_column_of(owner_list, norm_scale)
    adj_rows = adjoint_rows(my_waves, lat_plain, cotangent, owners * radii)
    adj_got = lax.all_to_all(adj_rows, ("ma", "row"), 0, 0, tiled=True)
    seed_rows = forward_rows(my_waves, lat_slots, owned_seed, owners * radii)
    seed_got = lax.all_to_all(seed_rows, ("ma", "row"), 0, 0, tiled=True)
    listed = list_seed(owned_seed)
    back_rows = grid_step(seed_got, adj_got, cosine, minus_sine, middle, radii)
    returned = lax.all_to_all(back_rows, ("ma", "row"), 0, 0, tiled=True)
    nonlinear, seed_next = results(step_size, my_waves, lat_plain, returned, listed)
    return (nonlinear, seed_next)


def local_small(seed_field, cotangent, step_size, owner_list):
    owner_count = lax.axis_size("ma")
    own_waves = cotangent.shape[3]
    norm_scale = 2.0 / math.sqrt(DEGREES * WAVES)
    block_width = min(128, WAVES)
    my_waves = lax.dynamic_slice_in_dim(owner_list, lax.axis_index("ma") * own_waves, own_waves)
    degree = jnp.arange(DEGREES, dtype=jnp.int32)
    live_cols = degree[:, None] >= my_waves[None, :]
    live_rows = jnp.transpose(live_cols)
    zero_value = jnp.zeros((), jnp.bfloat16)
    listed = jnp.take(seed_field, owner_list, axis=4)
    owned_seed = lax.all_to_all(listed, "ma", split_axis=4, concat_axis=3, tiled=True)
    lat_table = lat_cosines(jnp.arange(NLAT, dtype=jnp.int32))
    forward_rows = jnp.einsum(
        "crslk,tl->crstk",
        jnp.where(live_cols, owned_seed, zero_value),
        lat_table,
        preferred_element_type=jnp.float32,
    )
    adjoint_rows = jnp.einsum(
        "crskl,tl->crstk",
        jnp.where(live_rows, cotangent, zero_value),
        lat_table,
        preferred_element_type=jnp.float32,
    )
    spec_rows = jnp.concatenate([forward_rows, adjoint_rows], axis=0).astype(jnp.bfloat16)
    gridded = lax.all_to_all(
        lax.all_to_all(spec_rows, "ma", split_axis=3, concat_axis=4, tiled=True),
        "row",
        split_axis=3,
        concat_axis=1,
        tiled=True,
    )
    grid_field = None
    for start in range(0, WAVES, block_width):
        wave_block = wave_cosines(owner_list[start : start + block_width])
        partial_grid = jnp.einsum(
            "crsjm,smf->crjf",
            gridded[..., start : start + block_width],
            wave_block,
            preferred_element_type=jnp.float32,
        )
        grid_field = partial_grid if grid_field is None else grid_field + partial_grid
    grid_field = norm_scale * grid_field
    radial_pair = jnp.stack([grid_field[1], grid_field[3]])
    padded = jnp.pad(radial_pair, ((0, 0), (1, 1), (0, 0), (0, 0)))
    slopes = 0.5 * (padded[:, 2:] - padded[:, :-2])
    vel_tor = grid_field[0]
    mag_tor = grid_field[2]
    adj_vel = grid_field[4]
    adj_mag = grid_field[5]
    vel_pol = slopes[0]
    mag_pol = slopes[1]
    term_vel = mag_tor * mag_pol - vel_tor * vel_pol
    term_mag = vel_tor * mag_pol - vel_pol * mag_tor
    grad_vtor = -vel_pol * adj_vel + mag_pol * adj_mag
    grad_vpol = -vel_tor * adj_vel - mag_tor * adj_mag
    grad_mtor = mag_pol * adj_vel - vel_pol * adj_mag
    grad_mpol = mag_tor * adj_vel + vel_tor * adj_mag
    cotangent_pair = jnp.stack([grad_vpol, grad_mpol])
    padded_back = jnp.pad(cotangent_pair, ((0, 0), (1, 1), (0, 0), (0, 0)))
    back_slopes = 0.5 * (padded_back[:, :-2] - padded_back[:, 2:])
    analysis_in = jnp.stack(
        [term_vel, term_mag, grad_vtor, back_slopes[0], grad_mtor, back_slopes[1]]
    ).astype(jnp.bfloat16)
    spectra_parts = []
    for start in range(0, WAVES, block_width):
        wave_block = wave_cosines(owner_list[start : start + block_width])
        spectra_parts.append(
            jnp.einsum(
                "crjf,smf->crsjm", analysis_in, wave_block, preferred_element_type=jnp.float32
            )
        )
    spectra = (norm_scale * jnp.concatenate(spectra_parts, axis=4)).astype(jnp.bfloat16)
    position = jnp.arange(NLAT, dtype=jnp.int32)
    returned = lax.all_to_all(
        lax.all_to_all(spectra, "ma", split_axis=4, concat_axis=3, tiled=True),
        "row",
        split_axis=1,
        concat_axis=3,
        tiled=True,
    )
    sub_rows = spectra.shape[3]
    radial_part = position // (owner_count * sub_rows)
    owner_part = position // sub_rows % owner_count
    theta_index = owner_part * (NLAT // owner_count) + radial_part * sub_rows + position % sub_rows
    back_table = lat_cosines(theta_index)
    result = jnp.einsum("crstk,tl->crskl", returned, back_table, preferred_element_type=jnp.float32)
    result = jnp.where(live_rows, result, 0.0)
    nonlinear = result[:2]
    seed_next = jnp.swapaxes(owned_seed, 3, 4).astype(jnp.float32) - step_size[0] * result[2:]
    return (nonlinear, seed_next)


def fits(mesh):
    owners, radii = mesh.shape["ma"], mesh.shape["row"]
    own, sub = WAVES // owners, NLAT // (owners * radii)
    return own % 128 == 0 and sub % 16 == 0 and owners > 2 and owners & (owners - 1) == 0


def solution(mesh):
    return jax.shard_map(
        local if fits(mesh) else local_small,
        mesh=mesh,
        in_specs=(P(None, "row", None, "ma", None), P(None, "row", None, "ma", None), P(), P()),
        out_specs=(P(None, "row", None, "ma", None), P(None, "row", None, "ma", None)),
        check_vma=False,
    )
```
